512 devices in a mesh: cuts: 128 (over z, y, core), batch: 4 (over x).
Axes of the slice: x: 4, y: 8, z: 8, core: 2. Of those that a mesh axis runs over, the one named last changes fastest.
Arguments:
- blocks: bfloat16 [65536, 64, 128], P(('cuts', 'batch')), may hold values from -6 to 6
- environments: bfloat16 [65536, 64, 128], P(('cuts', 'batch')), may hold values from -0.5 to 0.5
- layers: bfloat16 [8, 64, 128], replicated, may hold values from -0.5 to 0.5
- selectors: bfloat16 [65536, 8, 128], P(('cuts', 'batch')), may hold values from -6 to 6
- classes: int32 [512, 128], P(('cuts', 'batch')), may hold values from 1 to 8
- routing: int32 [512, 128], P(('cuts', 'batch')), may hold values from 0 to 127, each once within a row
- left_edges: bfloat16 [64, 128], replicated, may hold values from -0.5 to 0.5
- right_edges: bfloat16 [64, 128], replicated, may hold values from -0.5 to 0.5
- owner_map: int32 [4096], replicated, may hold values from 0 to 4095, each once
Outputs:
- amplitudes: float32 [2, 4096], P(None, ('cuts', 'batch'))
The draws below stay inside these ranges and needn't reach their ends.
Inputs may be any that keep to these rules, and one draw needn't show every extreme that they name: `routing`: each holder's row is a permutation of 0 to 127. `owner_map`: A permutation of the bitstrings.
All inputs are finite; a program needn't handle non-finite values.
Results may differ from the reference program's by a relative error of at most 0.009.
Values may be sent and summed in bfloat16 or wider, within the bound.
No kernel may reach another device: no remote copies, remote signals or barrier semaphores. Data moves between devices by JAX's collectives and lax.ppermute only.
A program may use at most 64 MiB of HBM per device.

```python
import jax
import jax.numpy as jnp
from jax import lax

K = 64
HALF = 64
DEPTH = 8
GROUP = 1
SLOTS = 128
HOLDERS = 512
SLICES = 65536
BITS = 4096
N_CUTS = 128
N_BATCH = 4


def draw_classes(key, part):
    loaded = jax.random.randint(jax.random.fold_in(key, 11), (HOLDERS, 1), 0, 2)
    strong_levels = jax.random.randint(jax.random.fold_in(key, 12), (HOLDERS, SLOTS), DEPTH // 2 + 1, DEPTH + 1)
    light_levels = jax.random.randint(jax.random.fold_in(key, 13), (HOLDERS, SLOTS), 1, DEPTH // 2)
    return jnp.where(loaded == 1, strong_levels, light_levels).astype(jnp.int32)


def steps_of(stream_key, shape, pieces, smallest, top_value):
    level = 1.0
    for position, parts in pieces:
        heights = jax.random.uniform(jax.random.fold_in(jax.random.fold_in(stream_key, 6), position), (parts,), jnp.float32, smallest / len(pieces), top_value / len(pieces))
        level = level * jnp.repeat(jnp.exp(heights), shape[position] // parts).reshape((-1,) + (1,) * (len(shape) - 1 - position))
    return level


def gaussian(rng, dims, width, most, pieces=(), kind=jnp.bfloat16):
    array = jax.random.normal(rng, dims, jnp.float32) * width
    if len(pieces) > 0:
        array = steps_of(rng, dims, pieces, -0.22, 0.18) * array
    return jnp.clip(array, min=-most, max=most).astype(kind)


def setup_inputs(seed: int = 0) -> dict:
    seeds = jax.random.split(jax.random.key(seed), 10)
    return {
        "blocks": gaussian(seeds[0], (SLICES, K, 2 * K), 1.0, 6.0, ((0, 512),)),
        "environments": gaussian(seeds[1], (SLICES, K, 2 * K), (2 * K) ** -0.5, 0.5, ((0, 512),)),
        "layers": gaussian(seeds[2], (DEPTH, K, 2 * K), (2 * K) ** -0.5, 0.5),
        "selectors": gaussian(seeds[3], (SLICES, DEPTH, 2 * K), 0.7071, 6.0, ((0, 512),)),
        "classes": draw_classes(jax.random.fold_in(seeds[9], 71), 0),
        "routing": jax.vmap(lambda own: jax.random.permutation(own, SLOTS))(jax.random.split(seeds[5], HOLDERS)).reshape((HOLDERS, SLOTS)).astype(jnp.int32),
        "left_edges": gaussian(seeds[6], (K, 2 * HALF), (2 * K) ** -0.5, 0.5),
        "right_edges": gaussian(seeds[7], (K, 2 * HALF), (2 * K) ** -0.5, 0.5),
        "owner_map": jax.random.permutation(seeds[8], BITS).astype(jnp.int32),
    }


def block_form(matrix):
    half_count = matrix.shape[-1] // 2
    real_block = matrix[..., :half_count]
    imag_block = matrix[..., half_count:]
    upper_rows = jnp.concatenate([real_block, imag_block], axis=-1)
    lower_rows = jnp.concatenate([-imag_block, real_block], axis=-1)
    return jnp.concatenate([upper_rows, lower_rows], axis=-2)


def apply_phase(product, factors):
    half_count = product.shape[-1] // 2
    prod_real = product[..., :half_count]
    prod_imag = product[..., half_count:]
    fac_real = factors[..., :half_count].astype(jnp.float32)[:, None, :]
    fac_imag = factors[..., half_count:].astype(jnp.float32)[:, None, :]
    out_real = prod_real * fac_real - prod_imag * fac_imag
    out_imag = prod_real * fac_imag + prod_imag * fac_real
    return jnp.concatenate([out_real, out_imag], axis=-1)


def contract(worked, partners):
    slot_count, bond_width, doubled = worked.shape
    parted = worked.astype(jnp.float32).reshape(slot_count, bond_width, 2, bond_width)
    products = jnp.einsum('sipj,sjk->pik', parted, partners.astype(jnp.float32))
    real_part = products[0, :, :bond_width] - products[1, :, bond_width:]
    imag_part = products[0, :, bond_width:] + products[1, :, :bond_width]
    return real_part, imag_part


def amplitude_table(real_part, imag_part, left_edges, right_edges, owner_map):
    highest = lax.Precision.HIGHEST
    half_count = left_edges.shape[1] // 2
    left_real = left_edges[:, :half_count].astype(jnp.float32)
    left_imag = left_edges[:, half_count:].astype(jnp.float32)
    right_real = right_edges[:, :half_count].astype(jnp.float32)
    right_imag = right_edges[:, half_count:].astype(jnp.float32)
    wave_real = jnp.dot(real_part, right_real, precision=highest) - jnp.dot(imag_part, right_imag, precision=highest)
    wave_imag = jnp.dot(real_part, right_imag, precision=highest) + jnp.dot(imag_part, right_real, precision=highest)
    amp_real = jnp.dot(left_real.T, wave_real, precision=highest) - jnp.dot(left_imag.T, wave_imag, precision=highest)
    amp_imag = jnp.dot(left_real.T, wave_imag, precision=highest) + jnp.dot(left_imag.T, wave_real, precision=highest)
    flattened = jnp.stack([amp_real.reshape(-1), amp_imag.reshape(-1)])
    return flattened[:, owner_map]


def reference(blocks, environments, layers, selectors, classes, routing, left_edges, right_edges, owner_map):
    holders = N_CUTS * N_BATCH
    bond_width = blocks.shape[1]
    tables = block_form(layers).astype(jnp.float32)
    grouped = blocks.reshape(holders, SLOTS, bond_width, 2 * bond_width)
    factor_grid = selectors.reshape(holders, SLOTS, DEPTH, 2 * bond_width)
    partner_grid = environments.reshape(N_CUTS, N_BATCH, SLOTS, bond_width, 2 * bond_width)
    positions = jnp.arange(SLOTS, dtype=jnp.int32)
    targets = positions // GROUP
    within = positions % GROUP

    def one_holder(running, inputs):
        worked, factors, levels, sending, holder = inputs
        cut_index = holder // N_BATCH
        batch_index = holder % N_BATCH
        for layer_index in range(DEPTH):
            product = jnp.einsum('sij,jk->sik', worked.astype(jnp.float32), tables[layer_index])
            updated = apply_phase(product, factors[:, layer_index, :]).astype(jnp.bfloat16)
            worked = jnp.where((levels > layer_index)[:, None, None], updated, worked)
        outgoing = worked[sending]
        partners = partner_grid[targets, batch_index, cut_index * GROUP + within]
        real_part, imag_part = contract(outgoing, partners)
        return (running[0] + real_part, running[1] + imag_part), None

    start_value = (jnp.zeros((bond_width, bond_width), jnp.float32), jnp.zeros((bond_width, bond_width), jnp.float32))
    holder_ids = jnp.arange(holders, dtype=jnp.int32)
    totals, unused = lax.scan(one_holder, start_value, (grouped, factor_grid, classes, routing, holder_ids))
    amp_table = amplitude_table(totals[0], totals[1], left_edges, right_edges, owner_map)
    return amp_table * (SLICES ** -0.5)
```

```python
import jax
import jax.numpy as jnp
from jax import lax
from jax.experimental import pallas as pl
from jax.experimental.pallas import tpu as pltpu
from jax.sharding import Mesh
from jax.sharding import PartitionSpec as P

CUTS = ("cuts_0", "cuts_1", "cuts_2")
CUTS_BATCH = ("cuts_0", "cuts_1", "cuts_2", "batch")
PLANE = ("cuts_0", "cuts_1")
NEAR = ("cuts_2", "batch")
TOGETHER = 8


def lower_half(shape):
    return lax.broadcasted_iota(jnp.int32, shape, len(shape) - 1) < shape[-1] // 2


def times_i(matrix):
    turned = pltpu.roll(matrix, matrix.shape[-1] // 2, axis=matrix.ndim - 1)
    return jnp.where(lower_half(matrix.shape), -turned, turned)


def advance_kernel(
    levels, sending, blocks, selectors, layers, left, right, owners, packed, left_cols, right_cols, tables
):
    depth, bond, doubled = layers.shape
    slots = blocks.shape[0]
    for layer in range(depth):
        plain = layers[layer].astype(jnp.float32)
        turned = times_i(plain)
        tables[layer, :bond, :doubled] = plain.astype(jnp.bfloat16)
        tables[layer, :bond, doubled:] = turned.astype(jnp.bfloat16)
        tables[layer, bond:, :doubled] = turned.astype(jnp.bfloat16)
        tables[layer, bond:, doubled:] = (-plain).astype(jnp.bfloat16)

    def stacked(edges):
        return jnp.concatenate([edges[:, :bond], edges[:, bond:]], axis=0)

    left_rows = stacked(left[...])
    right_rows = stacked(right[...])
    width = 512

    def columns(step, carry):
        at = pl.ds(pl.multiple_of(step * width, width), width)
        owner = owners[:, at]
        codes = lax.broadcasted_iota(jnp.int32, (bond, width), 0)
        by_left = jnp.where(codes == owner // bond, 1.0, 0.0).astype(jnp.bfloat16)
        by_right = jnp.where(codes == owner % bond, 1.0, 0.0).astype(jnp.bfloat16)
        left_cols[:, at] = jnp.dot(left_rows, by_left, preferred_element_type=jnp.float32).astype(jnp.bfloat16)
        right_cols[:, at] = jnp.dot(right_rows, by_right, preferred_element_type=jnp.float32)
        return carry

    lax.fori_loop(0, owners.shape[1] // width, columns, 0)

    def group(index, carry):
        first = index * TOGETHER
        slot = [sending[0, first + k] for k in range(TOGETHER)]
        level = [levels[0, slot[k]] for k in range(TOGETHER)]
        current = [blocks[slot[k]] for k in range(TOGETHER)]
        straight, crossed = [], []
        for k in range(TOGETHER):
            factor = selectors[slot[k]].astype(jnp.float32)
            swapped = pltpu.roll(factor, bond, axis=1)
            mask = lower_half(factor.shape)
            straight.append(jnp.where(mask, factor, swapped))
            crossed.append(jnp.where(mask, swapped, factor))
        for layer in range(depth):
            product = jnp.dot(
                jnp.concatenate(current, axis=0), tables[layer], preferred_element_type=jnp.float32
            )
            for k in range(TOGETHER):
                rows = product[k * bond : (k + 1) * bond]
                updated = (
                    rows[:, :doubled] * straight[k][layer : layer + 1]
                    + rows[:, doubled:] * crossed[k][layer : layer + 1]
                )
                current[k] = lax.select(level[k] > layer, updated.astype(jnp.bfloat16), current[k])
        mask = lower_half((bond, doubled))
        for k in range(0, TOGETHER, 2):
            one = current[k].astype(jnp.float32)
            two = current[k + 1].astype(jnp.float32)
            real = jnp.where(mask, one, pltpu.roll(two, bond, axis=1)).astype(jnp.bfloat16)
            imag = jnp.where(mask, pltpu.roll(one, bond, axis=1), two).astype(jnp.bfloat16)
            quad, part = divmod(k, 4)
            lanes = slice(part * bond, part * bond + doubled)
            packed[index * (TOGETHER // 4) + quad, :bond, lanes] = real
            packed[index * (TOGETHER // 4) + quad, bond:, lanes] = imag
        return carry

    lax.fori_loop(0, slots // TOGETHER, group, 0)


def amplitude_kernel(packed, partners, left_cols, right_cols, partial, real_rows, imag_rows, *, scale):
    quads, doubled, depth = packed.shape
    bond = doubled // 2
    total = jnp.zeros((doubled, doubled), jnp.float32)
    for quad in range(quads):
        total = total + jnp.dot(packed[quad], partners[quad], preferred_element_type=jnp.float32)
    core = (total[:bond] + times_i(total[bond:])) * scale
    whole = jnp.concatenate([core, times_i(core)], axis=0)
    high = whole.astype(jnp.bfloat16)
    low = (whole - high.astype(jnp.float32)).astype(jnp.bfloat16)
    pieces = jnp.concatenate([high.astype(jnp.float32), low.astype(jnp.float32)], axis=0).T.astype(jnp.bfloat16)
    width = 512
    for start in range(0, left_cols.shape[1], width):
        cols = left_cols[:, start : start + width]
        half = jnp.dot(pieces, jnp.concatenate([cols, cols], axis=0), preferred_element_type=jnp.float32)
        half_real, half_imag = half[:bond], half[bond:]
        right_real = right_cols[:bond, start : start + width]
        right_imag = right_cols[bond:, start : start + width]
        real = jnp.sum(half_real * right_real - half_imag * right_imag, axis=0, keepdims=True)
        imag = jnp.sum(half_real * right_imag + half_imag * right_real, axis=0, keepdims=True)
        for tile in range(width // 128):
            row = start // 128 + tile
            real_rows[row : row + 1, :] = real[:, tile * 128 : (tile + 1) * 128]
            imag_rows[row : row + 1, :] = imag[:, tile * 128 : (tile + 1) * 128]
    real, imag = real_rows[...], imag_rows[...]
    first = lax.broadcasted_iota(jnp.int32, real.shape, 1) % 16 < 8
    half_rows = real.shape[0]
    partial[:half_rows] = jnp.where(first, real, pltpu.roll(imag, 8, axis=1))
    partial[half_rows:] = jnp.where(first, pltpu.roll(real, 120, axis=1), imag)


def fold_kernel(arrived, summed):
    summed[...] = jnp.broadcast_to(jnp.sum(arrived[...], axis=0, keepdims=True), summed.shape)


def finish_kernel(place, arrived, out):
    total = jnp.broadcast_to(jnp.sum(arrived[...], axis=0, keepdims=True), (8, 128))
    total = pltpu.roll(total, (128 - 16 * place[0]) % 128, axis=1)
    out[0:1, :] = total[0:1, 0:8]
    out[1:2, :] = total[0:1, 8:16]


VMEM = pl.BlockSpec(memory_space=pltpu.VMEM)
SMEM = pl.BlockSpec(memory_space=pltpu.SMEM)


def on_device(
    blocks, environments, layers, selectors, classes, routing, left_edges, right_edges, owner_map
):
    slots, bond, doubled = blocks.shape
    depth = layers.shape[0]
    bits = owner_map.shape[0]
    near = lax.axis_size(NEAR)
    plane = lax.axis_size(PLANE)
    partners = lax.all_to_all(environments, CUTS, split_axis=0, concat_axis=0, tiled=True)
    per = bits // (near * plane)
    owners = owner_map.reshape(2, plane // 2, near, per).transpose(1, 2, 0, 3).reshape(1, bits)
    packed, left_cols, right_cols = pl.pallas_call(
        advance_kernel,
        out_shape=(
            jax.ShapeDtypeStruct((slots // 4, doubled, 4 * bond), jnp.bfloat16),
            jax.ShapeDtypeStruct((doubled, bits), jnp.bfloat16),
            jax.ShapeDtypeStruct((doubled, bits), jnp.float32),
        ),
        in_specs=[SMEM, SMEM] + [VMEM] * 6,
        out_specs=(VMEM,) * 3,
        scratch_shapes=[pltpu.VMEM((depth, doubled, 2 * doubled), jnp.bfloat16)],
        compiler_params=pltpu.CompilerParams(vmem_limit_bytes=16 << 20),
        name="advance",
    )(classes, routing, blocks, selectors, layers, left_edges, right_edges, owners)
    rows = bits * 2 // doubled
    scale = float(slots * near * plane) ** -0.5
    partial = pl.pallas_call(
        lambda *refs: amplitude_kernel(*refs, scale=scale),
        out_shape=jax.ShapeDtypeStruct((rows, doubled), jnp.float32),
        in_specs=[VMEM] * 4,
        out_specs=VMEM,
        scratch_shapes=[pltpu.VMEM((rows // 2, doubled), jnp.float32)] * 2,
        compiler_params=pltpu.CompilerParams(vmem_limit_bytes=16 << 20),
        name="amplitudes",
    )(packed, partners.reshape(slots // 4, 4 * bond, doubled), left_cols, right_cols)
    arrived = lax.all_to_all(partial, PLANE, split_axis=0, concat_axis=0, tiled=True)
    summed = pl.pallas_call(
        fold_kernel,
        out_shape=jax.ShapeDtypeStruct((near, doubled), jnp.float32),
        in_specs=[VMEM],
        out_specs=VMEM,
        name="fold",
    )(arrived)
    arrived = lax.all_to_all(summed, NEAR, split_axis=0, concat_axis=0, tiled=True)
    place = lax.axis_index(NEAR).reshape(1).astype(jnp.int32)
    return pl.pallas_call(
        finish_kernel,
        out_shape=jax.ShapeDtypeStruct((2, per), jnp.float32),
        in_specs=[SMEM, VMEM],
        out_specs=VMEM,
        name="finish",
    )(place, arrived)


def solution(mesh):
    torus = Mesh(
        mesh.devices.reshape(8, 8, 2, mesh.shape["batch"]), ("cuts_0", "cuts_1", "cuts_2", "batch")
    )
    in_specs = (
        P(CUTS_BATCH, None, None),
        P(CUTS_BATCH, None, None),
        P(),
        P(CUTS_BATCH, None, None),
        P(CUTS_BATCH, None),
        P(CUTS_BATCH, None),
        P(),
        P(),
        P(),
    )
    out_specs = P(None, CUTS_BATCH)
    return jax.shard_map(
        on_device, mesh=torus, in_specs=in_specs, out_specs=out_specs, check_vma=False
    )
```

```python
import jax
import jax.numpy as jnp
from jax import lax
from jax.experimental import pallas as pl
from jax.experimental.pallas import tpu as pltpu
from jax.sharding import Mesh
from jax.sharding import PartitionSpec as P

CUTS = ("cuts_0", "cuts_1", "cuts_2")
CUTS_BATCH = ("cuts_0", "cuts_1", "cuts_2", "batch")
PLANE = ("cuts_0", "cuts_1")
NEAR = ("cuts_2", "batch")
TOGETHER = 8


def lower_half(shape):
    return lax.broadcasted_iota(jnp.int32, shape, len(shape) - 1) < shape[-1] // 2


def times_i(matrix):
    turned = pltpu.roll(matrix, matrix.shape[-1] // 2, axis=matrix.ndim - 1)
    return jnp.where(lower_half(matrix.shape), -turned, turned)


def advance_kernel(
    core, levels, sending, blocks, selectors, layers, left, right, owners,
    packed_other, packed_own, left_cols, right_cols, tables,
):
    depth, bond, doubled = layers.shape
    pairs = blocks.shape[0] // 2
    for layer in range(depth):
        plain = layers[layer].astype(jnp.float32)
        turned = times_i(plain)
        tables[layer, :bond, :doubled] = plain.astype(jnp.bfloat16)
        tables[layer, :bond, doubled:] = turned.astype(jnp.bfloat16)
        tables[layer, bond:, :doubled] = turned.astype(jnp.bfloat16)
        tables[layer, bond:, doubled:] = (-plain).astype(jnp.bfloat16)

    def stacked(edges):
        return jnp.concatenate([edges[:, :bond], edges[:, bond:]], axis=0)

    left_rows = stacked(left[...])
    right_rows = stacked(right[...])
    width = 512

    def columns(step, carry):
        at = pl.ds(pl.multiple_of(step * width, width), width)
        owner = owners[:, at]
        codes = lax.broadcasted_iota(jnp.int32, (bond, width), 0)
        by_left = jnp.where(codes == owner // bond, 1.0, 0.0).astype(jnp.bfloat16)
        by_right = jnp.where(codes == owner % bond, 1.0, 0.0).astype(jnp.bfloat16)
        left_cols[:, at] = jnp.dot(left_rows, by_left, preferred_element_type=jnp.float32).astype(jnp.bfloat16)
        right_cols[:, at] = jnp.dot(right_rows, by_right, preferred_element_type=jnp.float32).astype(jnp.bfloat16)
        return carry

    lax.fori_loop(0, owners.shape[1] // width, columns, 0)

    def group(index, carry, side, packed):
        first = index * TOGETHER
        slot = [sending[0, (first + k) * 2 + side] for k in range(TOGETHER)]
        level = [levels[0, slot[k]] for k in range(TOGETHER)]
        current = [blocks[slot[k]] for k in range(TOGETHER)]
        straight, crossed = [], []
        for k in range(TOGETHER):
            factor = selectors[slot[k]].astype(jnp.float32)
            swapped = pltpu.roll(factor, bond, axis=1)
            mask = lower_half(factor.shape)
            straight.append(jnp.where(mask, factor, swapped))
            crossed.append(jnp.where(mask, swapped, factor))
        for layer in range(depth):
            product = jnp.dot(
                jnp.concatenate(current, axis=0), tables[layer], preferred_element_type=jnp.float32
            )
            for k in range(TOGETHER):
                rows = product[k * bond : (k + 1) * bond]
                updated = (
                    rows[:, :doubled] * straight[k][layer : layer + 1]
                    + rows[:, doubled:] * crossed[k][layer : layer + 1]
                )
                current[k] = lax.select(level[k] > layer, updated.astype(jnp.bfloat16), current[k])
        mask = lower_half((bond, doubled))
        for k in range(0, TOGETHER, 2):
            one = current[k].astype(jnp.float32)
            two = current[k + 1].astype(jnp.float32)
            real = jnp.where(mask, one, pltpu.roll(two, bond, axis=1)).astype(jnp.bfloat16)
            imag = jnp.where(mask, pltpu.roll(one, bond, axis=1), two).astype(jnp.bfloat16)
            quad, part = divmod(k, 4)
            lanes = slice(part * bond, part * bond + doubled)
            packed[index * (TOGETHER // 4) + quad, :bond, lanes] = real
            packed[index * (TOGETHER // 4) + quad, bond:, lanes] = imag
        return carry

    steps = pairs // TOGETHER
    lax.fori_loop(0, steps, lambda i, c: group(i, c, 1 - core[0], packed_other), 0)
    lax.fori_loop(0, steps, lambda i, c: group(i, c, core[0], packed_own), 0)


def amplitude_kernel(
    core, own, other, partners_far, left_far, right_far, partial,
    partners, left_cols, right_cols, real_rows, imag_rows, arrivals, *, scale,
):
    quads, doubled, depth = own.shape
    bond = doubled // 2
    parts = 4
    each = quads // parts

    def load(part):
        at = pl.ds(part * each * 4, each * 4)
        return pltpu.make_async_copy(partners_far.at[at], partners.at[at], arrivals.at[part])

    for part in range(parts):
        load(part).start()
    edges = (
        pltpu.make_async_copy(left_far, left_cols, arrivals.at[parts]),
        pltpu.make_async_copy(right_far, right_cols, arrivals.at[parts + 1]),
    )
    for edge in edges:
        edge.start()
    total = jnp.zeros((doubled, doubled), jnp.float32)
    for part in range(parts):
        load(part).wait()
        for quad in range(part * each, (part + 1) * each):
            for worked, side in ((own, core[0]), (other, 1 - core[0])):
                rows = jnp.concatenate([partners[quad * 4 + k, side] for k in range(4)], axis=0)
                total = total + jnp.dot(worked[quad], rows, preferred_element_type=jnp.float32)
    core_matrix = (total[:bond] + times_i(total[bond:])) * scale
    whole = jnp.concatenate([core_matrix, times_i(core_matrix)], axis=0)
    high = whole.astype(jnp.bfloat16)
    low = (whole - high.astype(jnp.float32)).astype(jnp.bfloat16)
    pieces = jnp.concatenate([high.astype(jnp.float32), low.astype(jnp.float32)], axis=0).T.astype(jnp.bfloat16)
    width = 512
    for edge in edges:
        edge.wait()
    for start in range(0, left_cols.shape[1], width):
        cols = left_cols[:, start : start + width]
        half = jnp.dot(pieces, jnp.concatenate([cols, cols], axis=0), preferred_element_type=jnp.float32)
        half_real, half_imag = half[:bond], half[bond:]
        right_real = right_cols[:bond, start : start + width].astype(jnp.float32)
        right_imag = right_cols[bond:, start : start + width].astype(jnp.float32)
        real = jnp.sum(half_real * right_real - half_imag * right_imag, axis=0, keepdims=True)
        imag = jnp.sum(half_real * right_imag + half_imag * right_real, axis=0, keepdims=True)
        for tile in range(width // 128):
            row = start // 128 + tile
            real_rows[row : row + 1, :] = real[:, tile * 128 : (tile + 1) * 128]
            imag_rows[row : row + 1, :] = imag[:, tile * 128 : (tile + 1) * 128]
    real, imag = real_rows[...], imag_rows[...]
    first = lax.broadcasted_iota(jnp.int32, real.shape, 1) % 16 < 8
    half_rows = real.shape[0]
    partial[:half_rows] = jnp.where(first, real, pltpu.roll(imag, 8, axis=1))
    partial[half_rows:] = jnp.where(first, pltpu.roll(real, 120, axis=1), imag)


def fold_kernel(arrived, summed):
    summed[...] = jnp.broadcast_to(jnp.sum(arrived[...], axis=0, keepdims=True), summed.shape)


def finish_kernel(place, arrived, out):
    total = jnp.broadcast_to(jnp.sum(arrived[...], axis=0, keepdims=True), (8, 128))
    total = pltpu.roll(total, (128 - 16 * place[0]) % 128, axis=1)
    out[0:1, :] = total[0:1, 0:8]
    out[1:2, :] = total[0:1, 8:16]


VMEM = pl.BlockSpec(memory_space=pltpu.VMEM)
SMEM = pl.BlockSpec(memory_space=pltpu.SMEM)
FAR = pl.BlockSpec(memory_space=pltpu.HBM)


def on_device(
    blocks, environments, layers, selectors, classes, routing, left_edges, right_edges, owner_map
):
    slots, bond, doubled = blocks.shape
    depth = layers.shape[0]
    bits = owner_map.shape[0]
    near = lax.axis_size(NEAR)
    plane = lax.axis_size(PLANE)
    cores = lax.axis_size("cuts_2")
    partners = lax.all_to_all(
        environments.reshape(plane, cores * bond, doubled), PLANE, split_axis=0, concat_axis=0, tiled=True
    )
    core = lax.axis_index("cuts_2").reshape(1).astype(jnp.int32)
    place = lax.axis_index(NEAR).reshape(1).astype(jnp.int32)
    per = bits // (near * plane)
    owners = owner_map.reshape(2, plane // 2, near, per).transpose(1, 2, 0, 3).reshape(1, bits)
    core, place, owners = lax.optimization_barrier((core, place, owners))
    packed_other, packed_own, left_cols, right_cols = pl.pallas_call(
        advance_kernel,
        out_shape=(
            jax.ShapeDtypeStruct((plane // 4, doubled, 4 * bond), jnp.bfloat16),
            jax.ShapeDtypeStruct((plane // 4, doubled, 4 * bond), jnp.bfloat16),
            jax.ShapeDtypeStruct((doubled, bits), jnp.bfloat16),
            jax.ShapeDtypeStruct((doubled, bits), jnp.bfloat16),
        ),
        in_specs=[SMEM] * 3 + [VMEM] * 6,
        out_specs=(VMEM,) * 4,
        scratch_shapes=[pltpu.VMEM((depth, doubled, 2 * doubled), jnp.bfloat16)],
        compiler_params=pltpu.CompilerParams(vmem_limit_bytes=16 << 20),
        name="advance",
    )(core, classes, routing, blocks, selectors, layers, left_edges, right_edges, owners)
    received = lax.ppermute(packed_other, "cuts_2", [(0, 1), (1, 0)])
    rows = bits * 2 // doubled
    scale = float(slots * near * plane) ** -0.5
    partial = pl.pallas_call(
        lambda *refs: amplitude_kernel(*refs, scale=scale),
        out_shape=jax.ShapeDtypeStruct((rows, doubled), jnp.float32),
        in_specs=[SMEM, VMEM, VMEM, FAR, FAR, FAR],
        out_specs=VMEM,
        scratch_shapes=[
            pltpu.VMEM((plane, cores, bond, doubled), jnp.bfloat16),
            pltpu.VMEM((doubled, bits), jnp.bfloat16),
            pltpu.VMEM((doubled, bits), jnp.bfloat16),
            pltpu.VMEM((rows // 2, doubled), jnp.float32),
            pltpu.VMEM((rows // 2, doubled), jnp.float32),
            pltpu.SemaphoreType.DMA((6,)),
        ],
        compiler_params=pltpu.CompilerParams(vmem_limit_bytes=16 << 20),
        name="amplitudes",
    )(
        core,
        packed_own,
        received,
        pltpu.with_memory_space_constraint(partners.reshape(plane, cores, bond, doubled), pltpu.HBM),
        pltpu.with_memory_space_constraint(left_cols, pltpu.HBM),
        pltpu.with_memory_space_constraint(right_cols, pltpu.HBM),
    )
    arrived = lax.all_to_all(partial, PLANE, split_axis=0, concat_axis=0, tiled=True)
    summed = pl.pallas_call(
        fold_kernel,
        out_shape=jax.ShapeDtypeStruct((near, doubled), jnp.float32),
        in_specs=[VMEM],
        out_specs=VMEM,
        name="fold",
    )(pltpu.with_memory_space_constraint(arrived, pltpu.VMEM))
    arrived = lax.all_to_all(summed, NEAR, split_axis=0, concat_axis=0, tiled=True)
    return pl.pallas_call(
        finish_kernel,
        out_shape=jax.ShapeDtypeStruct((2, per), jnp.float32),
        in_specs=[SMEM, VMEM],
        out_specs=VMEM,
        name="finish",
    )(place, pltpu.with_memory_space_constraint(arrived, pltpu.VMEM))


def solution(mesh):
    torus = Mesh(
        mesh.devices.reshape(8, 8, 2, mesh.shape["batch"]), ("cuts_0", "cuts_1", "cuts_2", "batch")
    )
    in_specs = (
        P(CUTS_BATCH, None, None),
        P(CUTS_BATCH, None, None),
        P(),
        P(CUTS_BATCH, None, None),
        P(CUTS_BATCH, None),
        P(CUTS_BATCH, None),
        P(),
        P(),
        P(),
    )
    out_specs = P(None, CUTS_BATCH)
    return jax.shard_map(
        on_device, mesh=torus, in_specs=in_specs, out_specs=out_specs, check_vma=False
    )
```

```python
import jax
import jax.numpy as jnp
from jax import lax
from jax.experimental import pallas as pl
from jax.experimental.pallas import tpu as pltpu
from jax.sharding import Mesh
from jax.sharding import PartitionSpec as P

CUTS = ("cuts_0", "cuts_1", "cuts_2")
CUTS_BATCH = ("cuts_0", "cuts_1", "cuts_2", "batch")
PLANE = ("cuts_0", "cuts_1")
NEAR = ("cuts_2", "batch")
TOGETHER = 8


def lower_half(shape):
    return lax.broadcasted_iota(jnp.int32, shape, len(shape) - 1) < shape[-1] // 2


def times_i(matrix):
    turned = pltpu.roll(matrix, matrix.shape[-1] // 2, axis=matrix.ndim - 1)
    return jnp.where(lower_half(matrix.shape), -turned, turned)


def advance_kernel(
    core, levels, sending, blocks, selectors, layers, left, owners,
    packed_other, packed_own, left_cols, tables,
):
    depth, bond, doubled = layers.shape
    pairs = blocks.shape[0] // 2
    for layer in range(depth):
        plain = layers[layer].astype(jnp.float32)
        turned = times_i(plain)
        tables[layer, :bond, :doubled] = plain.astype(jnp.bfloat16)
        tables[layer, :bond, doubled:] = turned.astype(jnp.bfloat16)
        tables[layer, bond:, :doubled] = turned.astype(jnp.bfloat16)
        tables[layer, bond:, doubled:] = (-plain).astype(jnp.bfloat16)

    left_rows = jnp.concatenate([left[:, :bond], left[:, bond:]], axis=0)
    width = 512

    def columns(step, carry):
        at = pl.ds(pl.multiple_of(step * width, width), width)
        owner = owners[:, at]
        codes = lax.broadcasted_iota(jnp.int32, (bond, width), 0)
        by_left = jnp.where(codes == owner // bond, 1.0, 0.0).astype(jnp.bfloat16)
        left_cols[:, at] = jnp.dot(left_rows, by_left, preferred_element_type=jnp.float32).astype(jnp.bfloat16)
        return carry

    lax.fori_loop(0, owners.shape[1] // width, columns, 0)

    def group(index, carry, side, packed):
        first = index * TOGETHER
        slot = [sending[0, (first + k) * 2 + side] for k in range(TOGETHER)]
        level = [levels[0, slot[k]] for k in range(TOGETHER)]
        current = [blocks[slot[k]] for k in range(TOGETHER)]
        straight, crossed = [], []
        for k in range(TOGETHER):
            factor = selectors[slot[k]].astype(jnp.float32)
            swapped = pltpu.roll(factor, bond, axis=1)
            mask = lower_half(factor.shape)
            straight.append(jnp.where(mask, factor, swapped))
            crossed.append(jnp.where(mask, swapped, factor))
        for layer in range(depth):
            product = jnp.dot(
                jnp.concatenate(current, axis=0), tables[layer], preferred_element_type=jnp.float32
            )
            for k in range(TOGETHER):
                rows = product[k * bond : (k + 1) * bond]
                updated = (
                    rows[:, :doubled] * straight[k][layer : layer + 1]
                    + rows[:, doubled:] * crossed[k][layer : layer + 1]
                )
                current[k] = lax.select(level[k] > layer, updated.astype(jnp.bfloat16), current[k])
        mask = lower_half((bond, doubled))
        for k in range(0, TOGETHER, 2):
            one = current[k].astype(jnp.float32)
            two = current[k + 1].astype(jnp.float32)
            real = jnp.where(mask, one, pltpu.roll(two, bond, axis=1)).astype(jnp.bfloat16)
            imag = jnp.where(mask, pltpu.roll(one, bond, axis=1), two).astype(jnp.bfloat16)
            quad, part = divmod(k, 4)
            lanes = slice(part * bond, part * bond + doubled)
            packed[index * (TOGETHER // 4) + quad, :bond, lanes] = real
            packed[index * (TOGETHER // 4) + quad, bond:, lanes] = imag
        return carry

    steps = pairs // TOGETHER
    lax.fori_loop(0, steps, lambda i, c: group(i, c, 1 - core[0], packed_other), 0)
    lax.fori_loop(0, steps, lambda i, c: group(i, c, core[0], packed_own), 0)


def split(matrix):
    high = matrix.astype(jnp.bfloat16)
    return high, (matrix - high.astype(jnp.float32)).astype(jnp.bfloat16)


def amplitude_kernel(
    core, own, partners, owners, other_far, left_far, right_far, partial,
    other, left_cols, right, real_rows, imag_rows, arrivals, *, scale,
):
    quads, doubled, depth = own.shape
    bond = doubled // 2
    fetch_other = pltpu.make_async_copy(other_far, other, arrivals.at[0])
    fetch_left = pltpu.make_async_copy(left_far, left_cols, arrivals.at[1])
    fetch_right = pltpu.make_async_copy(right_far, right, arrivals.at[2])
    fetch_other.start()
    fetch_right.start()
    fetch_left.start()
    total = jnp.zeros((doubled, doubled), jnp.float32)
    for worked, side in ((own, core[0]), (other, 1 - core[0])):
        if worked is other:
            fetch_other.wait()
        for quad in range(quads):
            rows = jnp.concatenate([partners[quad * 4 + k, side] for k in range(4)], axis=0)
            total = total + jnp.dot(worked[quad], rows, preferred_element_type=jnp.float32)
    whole = (total[:bond] + times_i(total[bond:])) * scale
    fetch_right.wait()
    plain = right[...].astype(jnp.float32)
    factors = jnp.concatenate([plain, times_i(plain)], axis=0).astype(jnp.bfloat16)
    waves = jnp.dot(jnp.concatenate(split(whole), axis=0), factors, preferred_element_type=jnp.float32)
    wave = waves[:bond] + waves[bond:]
    high, low = split(jnp.concatenate([wave, times_i(wave)], axis=0))
    pieces = jnp.concatenate([high.astype(jnp.float32), low.astype(jnp.float32)], axis=0).T.astype(jnp.bfloat16)
    width = 512
    fetch_left.wait()
    for start in range(0, left_cols.shape[1], width):
        cols = left_cols[:, start : start + width]
        half = jnp.dot(pieces, jnp.concatenate([cols, cols], axis=0), preferred_element_type=jnp.float32)
        codes = lax.broadcasted_iota(jnp.int32, (bond, width), 0)
        chosen = codes == owners[:, start : start + width] % bond
        real = jnp.sum(jnp.where(chosen, half[:bond], 0.0), axis=0, keepdims=True)
        imag = jnp.sum(jnp.where(chosen, half[bond:], 0.0), axis=0, keepdims=True)
        for tile in range(width // 128):
            row = start // 128 + tile
            real_rows[row : row + 1, :] = real[:, tile * 128 : (tile + 1) * 128]
            imag_rows[row : row + 1, :] = imag[:, tile * 128 : (tile + 1) * 128]
    real, imag = real_rows[...], imag_rows[...]
    first = lax.broadcasted_iota(jnp.int32, real.shape, 1) % 16 < 8
    half_rows = real.shape[0]
    partial[:half_rows] = jnp.where(first, real, pltpu.roll(imag, 8, axis=1))
    partial[half_rows:] = jnp.where(first, pltpu.roll(real, 120, axis=1), imag)


def fold_kernel(arrived, summed):
    summed[...] = jnp.broadcast_to(jnp.sum(arrived[...], axis=0, keepdims=True), summed.shape)


def finish_kernel(place, arrived, out):
    total = jnp.broadcast_to(jnp.sum(arrived[...], axis=0, keepdims=True), (8, 128))
    total = pltpu.roll(total, (128 - 16 * place[0]) % 128, axis=1)
    out[0:1, :] = total[0:1, 0:8]
    out[1:2, :] = total[0:1, 8:16]


VMEM = pl.BlockSpec(memory_space=pltpu.VMEM)
SMEM = pl.BlockSpec(memory_space=pltpu.SMEM)
FAR = pl.BlockSpec(memory_space=pltpu.HBM)


def on_device(
    blocks, environments, layers, selectors, classes, routing, left_edges, right_edges, owner_map
):
    slots, bond, doubled = blocks.shape
    depth = layers.shape[0]
    bits = owner_map.shape[0]
    near = lax.axis_size(NEAR)
    plane = lax.axis_size(PLANE)
    cores = lax.axis_size("cuts_2")
    partners = lax.all_to_all(
        environments.reshape(plane, cores * bond, doubled), PLANE, split_axis=0, concat_axis=0, tiled=True
    )
    core = lax.axis_index("cuts_2").reshape(1).astype(jnp.int32)
    place = lax.axis_index(NEAR).reshape(1).astype(jnp.int32)
    per = bits // (near * plane)
    owners = owner_map.reshape(2, plane // 2, near, per).transpose(1, 2, 0, 3).reshape(1, bits)
    core, place, owners = lax.optimization_barrier((core, place, owners))
    packed_other, packed_own, left_cols = pl.pallas_call(
        advance_kernel,
        out_shape=(
            jax.ShapeDtypeStruct((plane // 4, doubled, 4 * bond), jnp.bfloat16),
            jax.ShapeDtypeStruct((plane // 4, doubled, 4 * bond), jnp.bfloat16),
            jax.ShapeDtypeStruct((doubled, bits), jnp.bfloat16),
        ),
        in_specs=[SMEM] * 3 + [VMEM] * 5,
        out_specs=(VMEM,) * 3,
        scratch_shapes=[pltpu.VMEM((depth, doubled, 2 * doubled), jnp.bfloat16)],
        compiler_params=pltpu.CompilerParams(vmem_limit_bytes=16 << 20),
        name="advance",
    )(core, classes, routing, blocks, selectors, layers, left_edges, owners)
    received = lax.ppermute(packed_other, "cuts_2", [(0, 1), (1, 0)])
    rows = bits * 2 // doubled
    scale = float(slots * near * plane) ** -0.5
    partial = pl.pallas_call(
        lambda *refs: amplitude_kernel(*refs, scale=scale),
        out_shape=jax.ShapeDtypeStruct((rows, doubled), jnp.float32),
        in_specs=[SMEM, VMEM, VMEM, VMEM, FAR, FAR, FAR],
        out_specs=VMEM,
        scratch_shapes=[
            pltpu.VMEM((plane // 4, doubled, 4 * bond), jnp.bfloat16),
            pltpu.VMEM((doubled, bits), jnp.bfloat16),
            pltpu.VMEM(right_edges.shape, jnp.bfloat16),
            pltpu.VMEM((rows // 2, doubled), jnp.float32),
            pltpu.VMEM((rows // 2, doubled), jnp.float32),
            pltpu.SemaphoreType.DMA((3,)),
        ],
        compiler_params=pltpu.CompilerParams(vmem_limit_bytes=16 << 20),
        name="amplitudes",
    )(
        core,
        packed_own,
        partners.reshape(plane, cores, bond, doubled),
        owners,
        pltpu.with_memory_space_constraint(received, pltpu.HBM),
        pltpu.with_memory_space_constraint(left_cols, pltpu.HBM),
        pltpu.with_memory_space_constraint(right_edges, pltpu.HBM),
    )
    arrived = lax.all_to_all(partial, PLANE, split_axis=0, concat_axis=0, tiled=True)
    summed = pl.pallas_call(
        fold_kernel,
        out_shape=jax.ShapeDtypeStruct((near, doubled), jnp.float32),
        in_specs=[VMEM],
        out_specs=VMEM,
        name="fold",
    )(pltpu.with_memory_space_constraint(arrived, pltpu.VMEM))
    arrived = lax.all_to_all(summed, NEAR, split_axis=0, concat_axis=0, tiled=True)
    return pl.pallas_call(
        finish_kernel,
        out_shape=jax.ShapeDtypeStruct((2, per), jnp.float32),
        in_specs=[SMEM, VMEM],
        out_specs=VMEM,
        name="finish",
    )(place, pltpu.with_memory_space_constraint(arrived, pltpu.VMEM))


def solution(mesh):
    torus = Mesh(
        mesh.devices.reshape(8, 8, 2, mesh.shape["batch"]), ("cuts_0", "cuts_1", "cuts_2", "batch")
    )
    in_specs = (
        P(CUTS_BATCH, None, None),
        P(CUTS_BATCH, None, None),
        P(),
        P(CUTS_BATCH, None, None),
        P(CUTS_BATCH, None),
        P(CUTS_BATCH, None),
        P(),
        P(),
        P(),
    )
    out_specs = P(None, CUTS_BATCH)
    return jax.shard_map(
        on_device, mesh=torus, in_specs=in_specs, out_specs=out_specs, check_vma=False
    )
```

```python
import jax
import jax.numpy as jnp
from jax import lax
from jax.experimental import pallas as pl
from jax.experimental.pallas import tpu as pltpu
from jax.sharding import Mesh
from jax.sharding import PartitionSpec as P

CUTS = ("cuts_0", "cuts_1", "cuts_2")
CUTS_BATCH = ("cuts_0", "cuts_1", "cuts_2", "batch")
PLANE = ("cuts_0", "cuts_1")
NEAR = ("cuts_2", "batch")
TOGETHER = 8
PARTS = 4


def lower_half(shape):
    return lax.broadcasted_iota(jnp.int32, shape, len(shape) - 1) < shape[-1] // 2


def times_i(matrix):
    turned = pltpu.roll(matrix, matrix.shape[-1] // 2, axis=matrix.ndim - 1)
    return jnp.where(lower_half(matrix.shape), -turned, turned)


def advance_kernel(
    core, levels, sending, blocks, selectors, layers, left, right, owners,
    packed_other, packed_own, left_cols, tables,
):
    depth, bond, doubled = layers.shape
    pairs = blocks.shape[0] // 2
    for layer in range(depth):
        plain = layers[layer].astype(jnp.float32)
        turned = times_i(plain)
        tables[layer, :bond, :doubled] = plain.astype(jnp.bfloat16)
        tables[layer, :bond, doubled:] = turned.astype(jnp.bfloat16)
        tables[layer, bond:, :doubled] = turned.astype(jnp.bfloat16)
        tables[layer, bond:, doubled:] = (-plain).astype(jnp.bfloat16)

    plain = right[...].astype(jnp.float32)
    packed_own[pairs // 4, :, :doubled] = jnp.concatenate([plain, times_i(plain)], axis=0).astype(jnp.bfloat16)
    left_rows = jnp.concatenate([left[:, :bond], left[:, bond:]], axis=0)
    width = 512

    def columns(step, carry):
        at = pl.ds(pl.multiple_of(step * width, width), width)
        owner = owners[:, at]
        codes = lax.broadcasted_iota(jnp.int32, (bond, width), 0)
        by_left = jnp.where(codes == owner // bond, 1.0, 0.0).astype(jnp.bfloat16)
        left_cols[:, at] = jnp.dot(left_rows, by_left, preferred_element_type=jnp.float32).astype(jnp.bfloat16)
        return carry

    lax.fori_loop(0, owners.shape[1] // width, columns, 0)

    def group(index, carry, side, packed):
        first = index * TOGETHER
        slot = [sending[0, (first + k) * 2 + side] for k in range(TOGETHER)]
        level = [levels[0, slot[k]] for k in range(TOGETHER)]
        current = [blocks[slot[k]] for k in range(TOGETHER)]
        straight, crossed = [], []
        for k in range(TOGETHER):
            factor = selectors[slot[k]].astype(jnp.float32)
            swapped = pltpu.roll(factor, bond, axis=1)
            mask = lower_half(factor.shape)
            straight.append(jnp.where(mask, factor, swapped))
            crossed.append(jnp.where(mask, swapped, factor))
        for layer in range(depth):
            product = jnp.dot(
                jnp.concatenate(current, axis=0), tables[layer], preferred_element_type=jnp.float32
            )
            for k in range(TOGETHER):
                rows = product[k * bond : (k + 1) * bond]
                updated = (
                    rows[:, :doubled] * straight[k][layer : layer + 1]
                    + rows[:, doubled:] * crossed[k][layer : layer + 1]
                )
                current[k] = lax.select(level[k] > layer, updated.astype(jnp.bfloat16), current[k])
        mask = lower_half((bond, doubled))
        for k in range(0, TOGETHER, 2):
            one = current[k].astype(jnp.float32)
            two = current[k + 1].astype(jnp.float32)
            real = jnp.where(mask, one, pltpu.roll(two, bond, axis=1)).astype(jnp.bfloat16)
            imag = jnp.where(mask, pltpu.roll(one, bond, axis=1), two).astype(jnp.bfloat16)
            quad, part = divmod(k, 4)
            lanes = slice(part * bond, part * bond + doubled)
            packed[index * (TOGETHER // 4) + quad, :bond, lanes] = real
            packed[index * (TOGETHER // 4) + quad, bond:, lanes] = imag
        return carry

    steps = pairs // TOGETHER
    lax.fori_loop(0, steps, lambda i, c: group(i, c, 1 - core[0], packed_other), 0)
    lax.fori_loop(0, steps, lambda i, c: group(i, c, core[0], packed_own), 0)


def split(matrix):
    high = matrix.astype(jnp.bfloat16)
    return high, (matrix - high.astype(jnp.float32)).astype(jnp.bfloat16)


def amplitude_kernel(
    core, own, partners, owners, other_far, left_far, partial,
    other, left_cols, real_rows, imag_rows, arrivals, *, scale,
):
    quads, doubled, depth = other.shape
    bond = doubled // 2
    for far, near, arrival in ((other_far, other, 0), (left_far, left_cols, 1)):
        each = near.shape[0] // PARTS
        for part in range(PARTS):
            at = pl.ds(part * each, each)
            pltpu.make_async_copy(far.at[at], near.at[at], arrivals.at[arrival]).start()
    total = jnp.zeros((doubled, doubled), jnp.float32)
    for worked, side in ((own, core[0]), (other, 1 - core[0])):
        if worked is other:
            pltpu.make_async_copy(other_far, other, arrivals.at[0]).wait()
        for quad in range(quads):
            rows = jnp.concatenate([partners[quad * 4 + k, side] for k in range(4)], axis=0)
            total = total + jnp.dot(worked[quad], rows, preferred_element_type=jnp.float32)
    whole = (total[:bond] + times_i(total[bond:])) * scale
    factors = own[quads, :, :doubled]
    waves = jnp.dot(jnp.concatenate(split(whole), axis=0), factors, preferred_element_type=jnp.float32)
    wave = waves[:bond] + waves[bond:]
    high, low = split(jnp.concatenate([wave, times_i(wave)], axis=0))
    pieces = jnp.concatenate([high.astype(jnp.float32), low.astype(jnp.float32)], axis=0).T.astype(jnp.bfloat16)
    width = 512
    pltpu.make_async_copy(left_far, left_cols, arrivals.at[1]).wait()
    for start in range(0, left_cols.shape[1], width):
        cols = left_cols[:, start : start + width]
        half = jnp.dot(pieces, jnp.concatenate([cols, cols], axis=0), preferred_element_type=jnp.float32)
        codes = lax.broadcasted_iota(jnp.int32, (bond, width), 0)
        chosen = codes == owners[:, start : start + width] % bond
        real = jnp.sum(jnp.where(chosen, half[:bond], 0.0), axis=0, keepdims=True)
        imag = jnp.sum(jnp.where(chosen, half[bond:], 0.0), axis=0, keepdims=True)
        for tile in range(width // 128):
            row = start // 128 + tile
            real_rows[row : row + 1, :] = real[:, tile * 128 : (tile + 1) * 128]
            imag_rows[row : row + 1, :] = imag[:, tile * 128 : (tile + 1) * 128]
    real, imag = real_rows[...], imag_rows[...]
    first = lax.broadcasted_iota(jnp.int32, real.shape, 1) % 16 < 8
    half_rows = real.shape[0]
    partial[:half_rows] = jnp.where(first, real, pltpu.roll(imag, 8, axis=1))
    partial[half_rows:] = jnp.where(first, pltpu.roll(real, 120, axis=1), imag)


def finish_kernel(place, arrived, out):
    total = jnp.broadcast_to(jnp.sum(arrived[...], axis=0, keepdims=True), (8, 128))
    total = pltpu.roll(total, (128 - 16 * place[0]) % 128, axis=1)
    out[0:1, :] = total[0:1, 0:8]
    out[1:2, :] = total[0:1, 8:16]


VMEM = pl.BlockSpec(memory_space=pltpu.VMEM)
SMEM = pl.BlockSpec(memory_space=pltpu.SMEM)
FAR = pl.BlockSpec(memory_space=pltpu.HBM)


def on_device(
    blocks, environments, layers, selectors, classes, routing, left_edges, right_edges, owner_map
):
    slots, bond, doubled = blocks.shape
    depth = layers.shape[0]
    bits = owner_map.shape[0]
    near = lax.axis_size(NEAR)
    plane = lax.axis_size(PLANE)
    cores = lax.axis_size("cuts_2")
    partners = lax.all_to_all(
        environments.reshape(plane, cores * bond, doubled), PLANE, split_axis=0, concat_axis=0, tiled=True
    )
    core = lax.axis_index("cuts_2").reshape(1).astype(jnp.int32)
    place = lax.axis_index(NEAR).reshape(1).astype(jnp.int32)
    per = bits // (near * plane)
    owners = owner_map.reshape(2, plane // 2, near, per).transpose(1, 2, 0, 3).reshape(1, bits)
    core, place, owners = lax.optimization_barrier((core, place, owners))
    packed_other, packed_own, left_cols = pl.pallas_call(
        advance_kernel,
        out_shape=(
            jax.ShapeDtypeStruct((plane // 4, doubled, 4 * bond), jnp.bfloat16),
            jax.ShapeDtypeStruct((plane // 4 + 1, doubled, 4 * bond), jnp.bfloat16),
            jax.ShapeDtypeStruct((doubled, bits), jnp.bfloat16),
        ),
        in_specs=[SMEM] * 3 + [VMEM] * 6,
        out_specs=(VMEM,) * 3,
        scratch_shapes=[pltpu.VMEM((depth, doubled, 2 * doubled), jnp.bfloat16)],
        compiler_params=pltpu.CompilerParams(vmem_limit_bytes=16 << 20),
        name="advance",
    )(core, classes, routing, blocks, selectors, layers, left_edges, right_edges, owners)
    received = lax.ppermute(packed_other, "cuts_2", [(0, 1), (1, 0)])
    rows = bits * 2 // doubled
    scale = float(slots * near * plane) ** -0.5
    partial = pl.pallas_call(
        lambda *refs: amplitude_kernel(*refs, scale=scale),
        out_shape=jax.ShapeDtypeStruct((rows, doubled), jnp.float32),
        in_specs=[SMEM, VMEM, VMEM, VMEM, FAR, FAR],
        out_specs=VMEM,
        scratch_shapes=[
            pltpu.VMEM((plane // 4, doubled, 4 * bond), jnp.bfloat16),
            pltpu.VMEM((doubled, bits), jnp.bfloat16),
            pltpu.VMEM((rows // 2, doubled), jnp.float32),
            pltpu.VMEM((rows // 2, doubled), jnp.float32),
            pltpu.SemaphoreType.DMA((2,)),
        ],
        compiler_params=pltpu.CompilerParams(vmem_limit_bytes=16 << 20),
        name="amplitudes",
    )(
        core,
        packed_own,
        partners.reshape(plane, cores, bond, doubled),
        owners,
        pltpu.with_memory_space_constraint(received, pltpu.HBM),
        pltpu.with_memory_space_constraint(left_cols, pltpu.HBM),
    )
    sent = jnp.broadcast_to(partial[:, None, :], (plane, near, doubled)).reshape(plane * near, doubled)
    arrived = lax.all_to_all(sent, CUTS_BATCH, split_axis=0, concat_axis=0, tiled=True)
    return pl.pallas_call(
        finish_kernel,
        out_shape=jax.ShapeDtypeStruct((2, per), jnp.float32),
        in_specs=[SMEM, VMEM],
        out_specs=VMEM,
        name="finish",
    )(place, pltpu.with_memory_space_constraint(arrived, pltpu.VMEM))


def solution(mesh):
    torus = Mesh(
        mesh.devices.reshape(8, 8, 2, mesh.shape["batch"]), ("cuts_0", "cuts_1", "cuts_2", "batch")
    )
    in_specs = (
        P(CUTS_BATCH, None, None),
        P(CUTS_BATCH, None, None),
        P(),
        P(CUTS_BATCH, None, None),
        P(CUTS_BATCH, None),
        P(CUTS_BATCH, None),
        P(),
        P(),
        P(),
    )
    out_specs = P(None, CUTS_BATCH)
    return jax.shard_map(
        on_device, mesh=torus, in_specs=in_specs, out_specs=out_specs, check_vma=False
    )
```

```python
import jax
import jax.numpy as jnp
from jax import lax
from jax.experimental import pallas as pl
from jax.experimental.pallas import tpu as pltpu
from jax.sharding import Mesh
from jax.sharding import PartitionSpec as P

CUTS = ("cuts_0", "cuts_1", "cuts_2")
CUTS_BATCH = ("cuts_0", "cuts_1", "cuts_2", "batch")
PLANE = ("cuts_0", "cuts_1")
NEAR = ("cuts_2", "batch")
TOGETHER = 8
PARTS = 4


def lower_half(shape):
    return lax.broadcasted_iota(jnp.int32, shape, len(shape) - 1) < shape[-1] // 2


def times_i(matrix):
    turned = pltpu.roll(matrix, matrix.shape[-1] // 2, axis=matrix.ndim - 1)
    return jnp.where(lower_half(matrix.shape), -turned, turned)


def advance_kernel(
    core, levels, sending, blocks, selectors, layers, left, right, owners,
    packed_other, packed_own, left_cols, tables,
):
    depth, bond, doubled = layers.shape
    pairs = blocks.shape[0] // 2
    for layer in range(depth):
        plain = layers[layer].astype(jnp.float32)
        turned = times_i(plain)
        tables[layer, :bond, :doubled] = plain.astype(jnp.bfloat16)
        tables[layer, :bond, doubled:] = turned.astype(jnp.bfloat16)
        tables[layer, bond:, :doubled] = turned.astype(jnp.bfloat16)
        tables[layer, bond:, doubled:] = (-plain).astype(jnp.bfloat16)

    plain = right[...].astype(jnp.float32)
    packed_own[pairs // 4, :, :doubled] = jnp.concatenate([plain, times_i(plain)], axis=0).astype(jnp.bfloat16)
    left_rows = jnp.concatenate([left[:, :bond], left[:, bond:]], axis=0)
    width = 512

    def columns(step, carry):
        at = pl.ds(pl.multiple_of(step * width, width), width)
        owner = owners[:, at]
        codes = lax.broadcasted_iota(jnp.int32, (bond, width), 0)
        by_left = jnp.where(codes == owner // bond, 1.0, 0.0).astype(jnp.bfloat16)
        left_cols[:, at] = jnp.dot(left_rows, by_left, preferred_element_type=jnp.float32).astype(jnp.bfloat16)
        return carry

    lax.fori_loop(0, owners.shape[1] // width, columns, 0)

    def group(index, carry, side, packed):
        first = index * TOGETHER
        slot = [sending[0, (first + k) * 2 + side] for k in range(TOGETHER)]
        level = [levels[0, slot[k]] for k in range(TOGETHER)]
        current = [blocks[slot[k]] for k in range(TOGETHER)]
        straight, crossed = [], []
        for k in range(TOGETHER):
            factor = selectors[slot[k]].astype(jnp.float32)
            swapped = pltpu.roll(factor, bond, axis=1)
            mask = lower_half(factor.shape)
            straight.append(jnp.where(mask, factor, swapped))
            crossed.append(jnp.where(mask, swapped, factor))
        for layer in range(depth):
            product = jnp.dot(
                jnp.concatenate(current, axis=0), tables[layer], preferred_element_type=jnp.float32
            )
            for k in range(TOGETHER):
                rows = product[k * bond : (k + 1) * bond]
                updated = (
                    rows[:, :doubled] * straight[k][layer : layer + 1]
                    + rows[:, doubled:] * crossed[k][layer : layer + 1]
                )
                current[k] = lax.select(level[k] > layer, updated.astype(jnp.bfloat16), current[k])
        mask = lower_half((bond, doubled))
        for k in range(0, TOGETHER, 2):
            one = current[k].astype(jnp.float32)
            two = current[k + 1].astype(jnp.float32)
            real = jnp.where(mask, one, pltpu.roll(two, bond, axis=1)).astype(jnp.bfloat16)
            imag = jnp.where(mask, pltpu.roll(one, bond, axis=1), two).astype(jnp.bfloat16)
            quad, part = divmod(k, 4)
            lanes = slice(part * bond, part * bond + doubled)
            packed[index * (TOGETHER // 4) + quad, :bond, lanes] = real
            packed[index * (TOGETHER // 4) + quad, bond:, lanes] = imag
        return carry

    steps = pairs // TOGETHER
    lax.fori_loop(0, steps, lambda i, c: group(i, c, 1 - core[0], packed_other), 0)
    lax.fori_loop(0, steps, lambda i, c: group(i, c, core[0], packed_own), 0)


def split(matrix):
    high = matrix.astype(jnp.bfloat16)
    return high, (matrix - high.astype(jnp.float32)).astype(jnp.bfloat16)


def amplitude_kernel(
    core, own, partners, owners, other_far, left_far, partial,
    other, left_cols, real_rows, imag_rows, arrivals, *, scale,
):
    quads, doubled, depth = other.shape
    bond = doubled // 2
    for far, near, arrival in ((other_far, other, 0), (left_far, left_cols, 1)):
        each = near.shape[0] // PARTS
        for part in range(PARTS):
            at = pl.ds(part * each, each)
            pltpu.make_async_copy(far.at[at], near.at[at], arrivals.at[arrival]).start()
    total = jnp.zeros((doubled, doubled), jnp.float32)
    for worked, side in ((own, core[0]), (other, 1 - core[0])):
        if worked is other:
            pltpu.make_async_copy(other_far, other, arrivals.at[0]).wait()
        for quad in range(quads):
            rows = jnp.concatenate([partners[quad * 4 + k, side] for k in range(4)], axis=0)
            total = total + jnp.dot(worked[quad], rows, preferred_element_type=jnp.float32)
    whole = (total[:bond] + times_i(total[bond:])) * scale
    factors = own[quads, :, :doubled]
    waves = jnp.dot(jnp.concatenate(split(whole), axis=0), factors, preferred_element_type=jnp.float32)
    wave = waves[:bond] + waves[bond:]
    high, low = split(jnp.concatenate([wave, times_i(wave)], axis=0))
    pieces = jnp.concatenate([high.astype(jnp.float32), low.astype(jnp.float32)], axis=0).T.astype(jnp.bfloat16)
    width = 512
    pltpu.make_async_copy(left_far, left_cols, arrivals.at[1]).wait()
    for start in range(0, left_cols.shape[1], width):
        cols = left_cols[:, start : start + width]
        half = jnp.dot(pieces, jnp.concatenate([cols, cols], axis=0), preferred_element_type=jnp.float32)
        codes = lax.broadcasted_iota(jnp.int32, (bond, width), 0)
        chosen = codes == owners[:, start : start + width] % bond
        real = jnp.sum(jnp.where(chosen, half[:bond], 0.0), axis=0, keepdims=True)
        imag = jnp.sum(jnp.where(chosen, half[bond:], 0.0), axis=0, keepdims=True)
        for tile in range(width // 128):
            row = start // 128 + tile
            real_rows[row : row + 1, :] = real[:, tile * 128 : (tile + 1) * 128]
            imag_rows[row : row + 1, :] = imag[:, tile * 128 : (tile + 1) * 128]
    real, imag = real_rows[...], imag_rows[...]
    first = lax.broadcasted_iota(jnp.int32, real.shape, 1) % 16 < 8
    half_rows = real.shape[0]
    partial[:half_rows] = jnp.where(first, real, pltpu.roll(imag, 8, axis=1))
    partial[half_rows:] = jnp.where(first, pltpu.roll(real, 120, axis=1), imag)


def fold_kernel(arrived, summed):
    total = jnp.sum(arrived[...], axis=0)
    summed[...] = jnp.broadcast_to(total[:, None, :], summed.shape)


def finish_kernel(place, arrived, out):
    total = jnp.broadcast_to(jnp.sum(arrived[...], axis=0, keepdims=True), (8, 128))
    total = pltpu.roll(total, (128 - 16 * place[0]) % 128, axis=1)
    out[0:1, :] = total[0:1, 0:8]
    out[1:2, :] = total[0:1, 8:16]


VMEM = pl.BlockSpec(memory_space=pltpu.VMEM)
SMEM = pl.BlockSpec(memory_space=pltpu.SMEM)
FAR = pl.BlockSpec(memory_space=pltpu.HBM)


def on_device(
    blocks, environments, layers, selectors, classes, routing, left_edges, right_edges, owner_map
):
    slots, bond, doubled = blocks.shape
    depth = layers.shape[0]
    bits = owner_map.shape[0]
    near = lax.axis_size(NEAR)
    plane = lax.axis_size(PLANE)
    cores = lax.axis_size("cuts_2")
    partners = lax.all_to_all(
        environments.reshape(plane, cores * bond, doubled), PLANE, split_axis=0, concat_axis=0, tiled=True
    )
    core = lax.axis_index("cuts_2").reshape(1).astype(jnp.int32)
    place = lax.axis_index("cuts_1").reshape(1).astype(jnp.int32)
    per = bits // (near * plane)
    columns = lax.axis_size("cuts_1")
    owners = owner_map.reshape(plane // columns, columns, near, per).transpose(2, 0, 1, 3)
    owners = owners.reshape(2, plane // 2, columns, per).transpose(1, 2, 0, 3).reshape(1, bits)
    core, place, owners = lax.optimization_barrier((core, place, owners))
    packed_other, packed_own, left_cols = pl.pallas_call(
        advance_kernel,
        out_shape=(
            jax.ShapeDtypeStruct((plane // 4, doubled, 4 * bond), jnp.bfloat16),
            jax.ShapeDtypeStruct((plane // 4 + 1, doubled, 4 * bond), jnp.bfloat16),
            jax.ShapeDtypeStruct((doubled, bits), jnp.bfloat16),
        ),
        in_specs=[SMEM] * 3 + [VMEM] * 6,
        out_specs=(VMEM,) * 3,
        scratch_shapes=[pltpu.VMEM((depth, doubled, 2 * doubled), jnp.bfloat16)],
        compiler_params=pltpu.CompilerParams(vmem_limit_bytes=16 << 20),
        name="advance",
    )(core, classes, routing, blocks, selectors, layers, left_edges, right_edges, owners)
    received = lax.ppermute(packed_other, "cuts_2", [(0, 1), (1, 0)])
    rows = bits * 2 // doubled
    scale = float(slots * near * plane) ** -0.5
    partial = pl.pallas_call(
        lambda *refs: amplitude_kernel(*refs, scale=scale),
        out_shape=jax.ShapeDtypeStruct((rows, doubled), jnp.float32),
        in_specs=[SMEM, VMEM, VMEM, VMEM, FAR, FAR],
        out_specs=VMEM,
        scratch_shapes=[
            pltpu.VMEM((plane // 4, doubled, 4 * bond), jnp.bfloat16),
            pltpu.VMEM((doubled, bits), jnp.bfloat16),
            pltpu.VMEM((rows // 2, doubled), jnp.float32),
            pltpu.VMEM((rows // 2, doubled), jnp.float32),
            pltpu.SemaphoreType.DMA((2,)),
        ],
        compiler_params=pltpu.CompilerParams(vmem_limit_bytes=16 << 20),
        name="amplitudes",
    )(
        core,
        packed_own,
        partners.reshape(plane, cores, bond, doubled),
        owners,
        pltpu.with_memory_space_constraint(received, pltpu.HBM),
        pltpu.with_memory_space_constraint(left_cols, pltpu.HBM),
    )
    arrived = lax.all_to_all(
        partial.reshape(near, rows // near, doubled), NEAR, split_axis=0, concat_axis=0, tiled=True
    )
    summed = pl.pallas_call(
        fold_kernel,
        out_shape=jax.ShapeDtypeStruct((plane // columns, columns, doubled), jnp.float32),
        in_specs=[VMEM],
        out_specs=VMEM,
        name="fold",
    )(pltpu.with_memory_space_constraint(arrived, pltpu.VMEM))
    arrived = lax.all_to_all(summed.reshape(plane, doubled), PLANE, split_axis=0, concat_axis=0, tiled=True)
    return pl.pallas_call(
        finish_kernel,
        out_shape=jax.ShapeDtypeStruct((2, per), jnp.float32),
        in_specs=[SMEM, VMEM],
        out_specs=VMEM,
        name="finish",
    )(place, pltpu.with_memory_space_constraint(arrived, pltpu.VMEM))


def solution(mesh):
    torus = Mesh(
        mesh.devices.reshape(8, 8, 2, mesh.shape["batch"]), ("cuts_0", "cuts_1", "cuts_2", "batch")
    )
    in_specs = (
        P(CUTS_BATCH, None, None),
        P(CUTS_BATCH, None, None),
        P(),
        P(CUTS_BATCH, None, None),
        P(CUTS_BATCH, None),
        P(CUTS_BATCH, None),
        P(),
        P(),
        P(),
    )
    out_specs = P(None, CUTS_BATCH)
    return jax.shard_map(
        on_device, mesh=torus, in_specs=in_specs, out_specs=out_specs, check_vma=False
    )
```

```python
import jax
import jax.numpy as jnp
from jax import lax
from jax.experimental import pallas as pl
from jax.experimental.pallas import tpu as pltpu
from jax.sharding import Mesh
from jax.sharding import PartitionSpec as P

CUTS = ("cuts_0", "cuts_1", "cuts_2")
CUTS_BATCH = ("cuts_0", "cuts_1", "cuts_2", "batch")
PLANE = ("cuts_0", "cuts_1")
NEAR = ("cuts_2", "batch")
TOGETHER = 8
PARTS = 4


def lower_half(shape):
    return lax.broadcasted_iota(jnp.int32, shape, len(shape) - 1) < shape[-1] // 2


def times_i(matrix):
    turned = pltpu.roll(matrix, matrix.shape[-1] // 2, axis=matrix.ndim - 1)
    return jnp.where(lower_half(matrix.shape), -turned, turned)


def advance_kernel(
    core, levels, sending, blocks, selectors, layers, left, right, owners,
    packed_other, packed_own, left_cols, tables,
):
    depth, bond, doubled = layers.shape
    pairs = blocks.shape[0] // 2
    for layer in range(depth):
        plain = layers[layer].astype(jnp.float32)
        turned = times_i(plain)
        tables[layer, :bond, :doubled] = plain.astype(jnp.bfloat16)
        tables[layer, :bond, doubled:] = turned.astype(jnp.bfloat16)
        tables[layer, bond:, :doubled] = turned.astype(jnp.bfloat16)
        tables[layer, bond:, doubled:] = (-plain).astype(jnp.bfloat16)

    plain = right[...].astype(jnp.float32)
    packed_own[pairs // 4, :, :doubled] = jnp.concatenate([plain, times_i(plain)], axis=0).astype(jnp.bfloat16)
    left_rows = jnp.concatenate([left[:, :bond], left[:, bond:]], axis=0)
    width = 512

    def columns(step, carry):
        at = pl.ds(pl.multiple_of(step * width, width), width)
        owner = owners[:, at]
        codes = lax.broadcasted_iota(jnp.int32, (bond, width), 0)
        by_left = jnp.where(codes == owner // bond, 1.0, 0.0).astype(jnp.bfloat16)
        left_cols[:, at] = jnp.dot(left_rows, by_left, preferred_element_type=jnp.float32).astype(jnp.bfloat16)
        return carry

    lax.fori_loop(0, owners.shape[1] // width, columns, 0)

    def group(index, carry, side, packed):
        first = index * TOGETHER
        slot = [sending[0, (first + k) * 2 + side] for k in range(TOGETHER)]
        level = [levels[0, slot[k]] for k in range(TOGETHER)]
        current = [blocks[slot[k]] for k in range(TOGETHER)]
        straight, crossed = [], []
        for k in range(TOGETHER):
            factor = selectors[slot[k]].astype(jnp.float32)
            swapped = pltpu.roll(factor, bond, axis=1)
            mask = lower_half(factor.shape)
            straight.append(jnp.where(mask, factor, swapped))
            crossed.append(jnp.where(mask, swapped, factor))
        for layer in range(depth):
            product = jnp.dot(
                jnp.concatenate(current, axis=0), tables[layer], preferred_element_type=jnp.float32
            )
            for k in range(TOGETHER):
                rows = product[k * bond : (k + 1) * bond]
                updated = (
                    rows[:, :doubled] * straight[k][layer : layer + 1]
                    + rows[:, doubled:] * crossed[k][layer : layer + 1]
                )
                current[k] = lax.select(level[k] > layer, updated.astype(jnp.bfloat16), current[k])
        mask = lower_half((bond, doubled))
        for k in range(0, TOGETHER, 2):
            one = current[k].astype(jnp.float32)
            two = current[k + 1].astype(jnp.float32)
            real = jnp.where(mask, one, pltpu.roll(two, bond, axis=1)).astype(jnp.bfloat16)
            imag = jnp.where(mask, pltpu.roll(one, bond, axis=1), two).astype(jnp.bfloat16)
            quad, part = divmod(k, 4)
            lanes = slice(part * bond, part * bond + doubled)
            packed[index * (TOGETHER // 4) + quad, :bond, lanes] = real
            packed[index * (TOGETHER // 4) + quad, bond:, lanes] = imag
        return carry

    steps = pairs // TOGETHER
    lax.fori_loop(0, steps, lambda i, c: group(i, c, 1 - core[0], packed_other), 0)
    lax.fori_loop(0, steps, lambda i, c: group(i, c, core[0], packed_own), 0)


def split(matrix):
    high = matrix.astype(jnp.bfloat16)
    return high, (matrix - high.astype(jnp.float32)).astype(jnp.bfloat16)


def amplitude_kernel(
    core, own, partners, owners, other_far, left_far, partial,
    other, left_cols, real_rows, imag_rows, arrivals, *, scale,
):
    quads, doubled, depth = other.shape
    bond = doubled // 2
    for far, near, arrival in ((other_far, other, 0), (left_far, left_cols, 1)):
        each = near.shape[0] // PARTS
        for part in range(PARTS):
            at = pl.ds(part * each, each)
            pltpu.make_async_copy(far.at[at], near.at[at], arrivals.at[arrival]).start()
    total = jnp.zeros((doubled, doubled), jnp.float32)
    for worked, side in ((own, core[0]), (other, 1 - core[0])):
        if worked is other:
            pltpu.make_async_copy(other_far, other, arrivals.at[0]).wait()
        for quad in range(quads):
            rows = jnp.concatenate([partners[quad * 4 + k, side] for k in range(4)], axis=0)
            total = total + jnp.dot(worked[quad], rows, preferred_element_type=jnp.float32)
    whole = (total[:bond] + times_i(total[bond:])) * scale
    factors = own[quads, :, :doubled]
    waves = jnp.dot(jnp.concatenate(split(whole), axis=0), factors, preferred_element_type=jnp.float32)
    wave = waves[:bond] + waves[bond:]
    high, low = split(jnp.concatenate([wave, times_i(wave)], axis=0))
    pieces = jnp.concatenate([high.astype(jnp.float32), low.astype(jnp.float32)], axis=0).T.astype(jnp.bfloat16)
    width = 512
    pltpu.make_async_copy(left_far, left_cols, arrivals.at[1]).wait()
    for start in range(0, left_cols.shape[1], width):
        cols = left_cols[:, start : start + width]
        half = jnp.dot(pieces, jnp.concatenate([cols, cols], axis=0), preferred_element_type=jnp.float32)
        codes = lax.broadcasted_iota(jnp.int32, (bond, width), 0)
        chosen = codes == owners[:, start : start + width] % bond
        real = jnp.sum(jnp.where(chosen, half[:bond], 0.0), axis=0, keepdims=True)
        imag = jnp.sum(jnp.where(chosen, half[bond:], 0.0), axis=0, keepdims=True)
        for tile in range(width // 128):
            row = start // 128 + tile
            real_rows[row : row + 1, :] = real[:, tile * 128 : (tile + 1) * 128]
            imag_rows[row : row + 1, :] = imag[:, tile * 128 : (tile + 1) * 128]
    real, imag = real_rows[...], imag_rows[...]
    first = lax.broadcasted_iota(jnp.int32, real.shape, 1) % 16 < 8
    half_rows = real.shape[0]
    partial[:half_rows] = jnp.where(first, real, pltpu.roll(imag, 8, axis=1))
    partial[half_rows:] = jnp.where(first, pltpu.roll(real, 120, axis=1), imag)


def fold_kernel(arrived, summed):
    total = jnp.sum(arrived[...], axis=0)
    summed[...] = jnp.broadcast_to(total[:, None, :], summed.shape)


def finish_kernel(place, arrived, out):
    total = jnp.broadcast_to(jnp.sum(arrived[...], axis=0, keepdims=True), (8, 128))
    total = pltpu.roll(total, (128 - 16 * place[0]) % 128, axis=1)
    out[0:1, :] = total[0:1, 0:8]
    out[1:2, :] = total[0:1, 8:16]


VMEM = pl.BlockSpec(memory_space=pltpu.VMEM)
SMEM = pl.BlockSpec(memory_space=pltpu.SMEM)
FAR = pl.BlockSpec(memory_space=pltpu.HBM)


def on_device(
    blocks, environments, layers, selectors, classes, routing, left_edges, right_edges, owner_map
):
    slots, bond, doubled = blocks.shape
    depth = layers.shape[0]
    bits = owner_map.shape[0]
    near = lax.axis_size(NEAR)
    plane = lax.axis_size(PLANE)
    cores = lax.axis_size("cuts_2")
    partners = lax.all_to_all(
        environments.reshape(plane, cores * bond, doubled), PLANE, split_axis=0, concat_axis=0, tiled=True
    )
    core = lax.axis_index("cuts_2").reshape(1).astype(jnp.int32)
    place = lax.axis_index("cuts_1").reshape(1).astype(jnp.int32)
    per = bits // (near * plane)
    columns = lax.axis_size("cuts_1")
    half = plane // columns // 2
    owners = owner_map.reshape(2, half * columns * near * per)[::-1]
    owners = owners.reshape(plane // columns, columns, near, per).transpose(2, 0, 1, 3)
    owners = owners.reshape(2, plane // 2, columns, per).transpose(1, 2, 0, 3).reshape(1, bits)
    core, place, owners = lax.optimization_barrier((core, place, owners))
    packed_other, packed_own, left_cols = pl.pallas_call(
        advance_kernel,
        out_shape=(
            jax.ShapeDtypeStruct((plane // 4, doubled, 4 * bond), jnp.bfloat16),
            jax.ShapeDtypeStruct((plane // 4 + 1, doubled, 4 * bond), jnp.bfloat16),
            jax.ShapeDtypeStruct((doubled, bits), jnp.bfloat16),
        ),
        in_specs=[SMEM] * 3 + [VMEM] * 6,
        out_specs=(VMEM,) * 3,
        scratch_shapes=[pltpu.VMEM((depth, doubled, 2 * doubled), jnp.bfloat16)],
        compiler_params=pltpu.CompilerParams(vmem_limit_bytes=16 << 20),
        name="advance",
    )(core, classes, routing, blocks, selectors, layers, left_edges, right_edges, owners)
    received = lax.ppermute(packed_other, "cuts_2", [(0, 1), (1, 0)])
    rows = bits * 2 // doubled
    scale = float(slots * near * plane) ** -0.5
    partial = pl.pallas_call(
        lambda *refs: amplitude_kernel(*refs, scale=scale),
        out_shape=jax.ShapeDtypeStruct((rows, doubled), jnp.float32),
        in_specs=[SMEM, VMEM, VMEM, VMEM, FAR, FAR],
        out_specs=VMEM,
        scratch_shapes=[
            pltpu.VMEM((plane // 4, doubled, 4 * bond), jnp.bfloat16),
            pltpu.VMEM((doubled, bits), jnp.bfloat16),
            pltpu.VMEM((rows // 2, doubled), jnp.float32),
            pltpu.VMEM((rows // 2, doubled), jnp.float32),
            pltpu.SemaphoreType.DMA((2,)),
        ],
        compiler_params=pltpu.CompilerParams(vmem_limit_bytes=16 << 20),
        name="amplitudes",
    )(
        core,
        packed_own,
        partners.reshape(plane, cores, bond, doubled),
        owners,
        pltpu.with_memory_space_constraint(received, pltpu.HBM),
        pltpu.with_memory_space_constraint(left_cols, pltpu.HBM),
    )
    arrived = lax.all_to_all(
        partial.reshape(near, rows // near, doubled), NEAR, split_axis=0, concat_axis=0, tiled=True
    )
    summed = pl.pallas_call(
        fold_kernel,
        out_shape=jax.ShapeDtypeStruct((plane // columns, columns, doubled), jnp.float32),
        in_specs=[VMEM],
        out_specs=VMEM,
        name="fold",
    )(pltpu.with_memory_space_constraint(arrived, pltpu.VMEM))
    far_first = [
        (row + half) % (2 * half) * columns + (column + columns // 2) % columns
        for row in range(2 * half)
        for column in range(columns)
    ]
    arrived = lax.all_to_all(
        summed.reshape(plane, doubled),
        PLANE,
        split_axis=0,
        concat_axis=0,
        tiled=True,
        axis_index_groups=[far_first],
    )
    return pl.pallas_call(
        finish_kernel,
        out_shape=jax.ShapeDtypeStruct((2, per), jnp.float32),
        in_specs=[SMEM, VMEM],
        out_specs=VMEM,
        name="finish",
    )(place, pltpu.with_memory_space_constraint(arrived, pltpu.VMEM))


def solution(mesh):
    torus = Mesh(
        mesh.devices.reshape(8, 8, 2, mesh.shape["batch"]), ("cuts_0", "cuts_1", "cuts_2", "batch")
    )
    in_specs = (
        P(CUTS_BATCH, None, None),
        P(CUTS_BATCH, None, None),
        P(),
        P(CUTS_BATCH, None, None),
        P(CUTS_BATCH, None),
        P(CUTS_BATCH, None),
        P(),
        P(),
        P(),
    )
    out_specs = P(None, CUTS_BATCH)
    return jax.shard_map(
        on_device, mesh=torus, in_specs=in_specs, out_specs=out_specs, check_vma=False
    )
```

```python
import jax
import jax.numpy as jnp
from jax import lax
from jax.experimental import pallas as pl
from jax.experimental.pallas import tpu as pltpu
from jax.sharding import Mesh
from jax.sharding import PartitionSpec as P

CUTS = ("cuts_0", "cuts_1", "cuts_2")
CUTS_BATCH = ("cuts_0", "cuts_1", "cuts_2", "batch")
PLANE = ("cuts_0", "cuts_1")
NEAR = ("cuts_2", "batch")
TOGETHER = 8
PARTS = 4


def lower_half(shape):
    return lax.broadcasted_iota(jnp.int32, shape, len(shape) - 1) < shape[-1] // 2


def times_i(matrix):
    turned = pltpu.roll(matrix, matrix.shape[-1] // 2, axis=matrix.ndim - 1)
    return jnp.where(lower_half(matrix.shape), -turned, turned)


def advance_kernel(
    core, levels, sending, blocks, selectors, layers, left, right, owners,
    packed_other, packed_own, left_cols, tables,
):
    depth, bond, doubled = layers.shape
    pairs = blocks.shape[0] // 2
    for layer in range(depth):
        plain = layers[layer].astype(jnp.float32)
        turned = times_i(plain)
        tables[layer, :bond, :doubled] = plain.astype(jnp.bfloat16)
        tables[layer, :bond, doubled:] = turned.astype(jnp.bfloat16)
        tables[layer, bond:, :doubled] = turned.astype(jnp.bfloat16)
        tables[layer, bond:, doubled:] = (-plain).astype(jnp.bfloat16)

    plain = right[...].astype(jnp.float32)
    packed_own[pairs // 4, :, :doubled] = jnp.concatenate([plain, times_i(plain)], axis=0).astype(jnp.bfloat16)
    left_rows = jnp.concatenate([left[:, :bond], left[:, bond:]], axis=0)
    width = 512

    def columns(step, carry):
        at = pl.ds(pl.multiple_of(step * width, width), width)
        owner = owners[:, at]
        codes = lax.broadcasted_iota(jnp.int32, (bond, width), 0)
        by_left = jnp.where(codes == owner // bond, 1.0, 0.0).astype(jnp.bfloat16)
        left_cols[:, at] = jnp.dot(left_rows, by_left, preferred_element_type=jnp.float32).astype(jnp.bfloat16)
        return carry

    lax.fori_loop(0, owners.shape[1] // width, columns, 0)

    def group(index, carry, side, packed):
        first = index * TOGETHER
        slot = [sending[0, (first + k) * 2 + side] for k in range(TOGETHER)]
        level = [levels[0, slot[k]] for k in range(TOGETHER)]
        current = [blocks[slot[k]] for k in range(TOGETHER)]
        straight, crossed = [], []
        for k in range(TOGETHER):
            factor = selectors[slot[k]].astype(jnp.float32)
            swapped = pltpu.roll(factor, bond, axis=1)
            mask = lower_half(factor.shape)
            straight.append(jnp.where(mask, factor, swapped))
            crossed.append(jnp.where(mask, swapped, factor))
        for layer in range(depth):
            product = jnp.dot(
                jnp.concatenate(current, axis=0), tables[layer], preferred_element_type=jnp.float32
            )
            for k in range(TOGETHER):
                rows = product[k * bond : (k + 1) * bond]
                updated = (
                    rows[:, :doubled] * straight[k][layer : layer + 1]
                    + rows[:, doubled:] * crossed[k][layer : layer + 1]
                )
                current[k] = lax.select(level[k] > layer, updated.astype(jnp.bfloat16), current[k])
        mask = lower_half((bond, doubled))
        for k in range(0, TOGETHER, 2):
            one = current[k].astype(jnp.float32)
            two = current[k + 1].astype(jnp.float32)
            real = jnp.where(mask, one, pltpu.roll(two, bond, axis=1)).astype(jnp.bfloat16)
            imag = jnp.where(mask, pltpu.roll(one, bond, axis=1), two).astype(jnp.bfloat16)
            quad, part = divmod(k, 4)
            lanes = slice(part * bond, part * bond + doubled)
            packed[index * (TOGETHER // 4) + quad, :bond, lanes] = real
            packed[index * (TOGETHER // 4) + quad, bond:, lanes] = imag
        return carry

    steps = pairs // TOGETHER
    lax.fori_loop(0, steps, lambda i, c: group(i, c, 1 - core[0], packed_other), 0)
    lax.fori_loop(0, steps, lambda i, c: group(i, c, core[0], packed_own), 0)


def split(matrix):
    high = matrix.astype(jnp.bfloat16)
    return high, (matrix - high.astype(jnp.float32)).astype(jnp.bfloat16)


def amplitude_kernel(
    core, own, partners, owners, other_far, left_far, partial,
    other, left_cols, real_rows, imag_rows, arrivals, *, scale,
):
    quads, doubled, depth = other.shape
    bond = doubled // 2
    for far, near, arrival in ((other_far, other, 0), (left_far, left_cols, 1)):
        each = near.shape[0] // PARTS
        for part in range(PARTS):
            at = pl.ds(part * each, each)
            pltpu.make_async_copy(far.at[at], near.at[at], arrivals.at[arrival]).start()
    total = jnp.zeros((doubled, doubled), jnp.float32)
    for worked, side in ((own, core[0]), (other, 1 - core[0])):
        if worked is other:
            pltpu.make_async_copy(other_far, other, arrivals.at[0]).wait()
        for quad in range(quads):
            rows = jnp.concatenate([partners[quad * 4 + k, side] for k in range(4)], axis=0)
            total = total + jnp.dot(worked[quad], rows, preferred_element_type=jnp.float32)
    whole = (total[:bond] + times_i(total[bond:])) * scale
    factors = own[quads, :, :doubled]
    waves = jnp.dot(jnp.concatenate(split(whole), axis=0), factors, preferred_element_type=jnp.float32)
    wave = waves[:bond] + waves[bond:]
    high, low = split(jnp.concatenate([wave, times_i(wave)], axis=0))
    pieces = jnp.concatenate([high.astype(jnp.float32), low.astype(jnp.float32)], axis=0).T.astype(jnp.bfloat16)
    width = 512
    pltpu.make_async_copy(left_far, left_cols, arrivals.at[1]).wait()
    for start in range(0, left_cols.shape[1], width):
        cols = left_cols[:, start : start + width]
        half = jnp.dot(pieces, jnp.concatenate([cols, cols], axis=0), preferred_element_type=jnp.float32)
        codes = lax.broadcasted_iota(jnp.int32, (bond, width), 0)
        chosen = codes == owners[:, start : start + width] % bond
        real = jnp.sum(jnp.where(chosen, half[:bond], 0.0), axis=0, keepdims=True)
        imag = jnp.sum(jnp.where(chosen, half[bond:], 0.0), axis=0, keepdims=True)
        for tile in range(width // 128):
            row = start // 128 + tile
            real_rows[row : row + 1, :] = real[:, tile * 128 : (tile + 1) * 128]
            imag_rows[row : row + 1, :] = imag[:, tile * 128 : (tile + 1) * 128]
    real, imag = real_rows[...], imag_rows[...]
    first = lax.broadcasted_iota(jnp.int32, real.shape, 1) % 16 < 8
    half_rows = real.shape[0]
    partial[:half_rows] = jnp.where(first, real, pltpu.roll(imag, 8, axis=1))
    partial[half_rows:] = jnp.where(first, pltpu.roll(real, 120, axis=1), imag)


def fold_kernel(arrived, summed):
    total = jnp.sum(arrived[...], axis=0)
    summed[...] = jnp.broadcast_to(total[:, None, :], summed.shape)


def finish_kernel(place, arrived, out):
    total = jnp.broadcast_to(jnp.sum(arrived[...], axis=0, keepdims=True), (8, 128))
    total = pltpu.roll(total, (128 - 16 * place[0]) % 128, axis=1)
    out[0:1, :] = total[0:1, 0:8]
    out[1:2, :] = total[0:1, 8:16]


VMEM = pl.BlockSpec(memory_space=pltpu.VMEM)
SMEM = pl.BlockSpec(memory_space=pltpu.SMEM)
FAR = pl.BlockSpec(memory_space=pltpu.HBM)


def on_device(
    blocks, environments, layers, selectors, classes, routing, left_edges, right_edges, owner_map
):
    slots, bond, doubled = blocks.shape
    depth = layers.shape[0]
    bits = owner_map.shape[0]
    near = lax.axis_size(NEAR)
    plane = lax.axis_size(PLANE)
    cores = lax.axis_size("cuts_2")
    partners = lax.all_to_all(
        environments.reshape(plane, cores * bond, doubled), PLANE, split_axis=0, concat_axis=0, tiled=True
    )
    core = lax.axis_index("cuts_2").reshape(1).astype(jnp.int32)
    place = lax.axis_index("cuts_1").reshape(1).astype(jnp.int32)
    per = bits // (near * plane)
    columns = lax.axis_size("cuts_1")
    half = plane // columns // 2
    owners = owner_map.reshape(2, half * columns * near * per)[::-1]
    owners = owners.reshape(plane, 2 * cores, near // cores // 2 * per)[:, ::-1]
    owners = owners.reshape(plane // columns, columns, near, per).transpose(2, 0, 1, 3)
    owners = owners.reshape(2, plane // 2, columns, per).transpose(1, 2, 0, 3).reshape(1, bits)
    core, place, owners = lax.optimization_barrier((core, place, owners))
    packed_other, packed_own, left_cols = pl.pallas_call(
        advance_kernel,
        out_shape=(
            jax.ShapeDtypeStruct((plane // 4, doubled, 4 * bond), jnp.bfloat16),
            jax.ShapeDtypeStruct((plane // 4 + 1, doubled, 4 * bond), jnp.bfloat16),
            jax.ShapeDtypeStruct((doubled, bits), jnp.bfloat16),
        ),
        in_specs=[SMEM] * 3 + [VMEM] * 6,
        out_specs=(VMEM,) * 3,
        scratch_shapes=[pltpu.VMEM((depth, doubled, 2 * doubled), jnp.bfloat16)],
        compiler_params=pltpu.CompilerParams(vmem_limit_bytes=16 << 20),
        name="advance",
    )(core, classes, routing, blocks, selectors, layers, left_edges, right_edges, owners)
    received = lax.ppermute(packed_other, "cuts_2", [(0, 1), (1, 0)])
    rows = bits * 2 // doubled
    scale = float(slots * near * plane) ** -0.5
    partial = pl.pallas_call(
        lambda *refs: amplitude_kernel(*refs, scale=scale),
        out_shape=jax.ShapeDtypeStruct((rows, doubled), jnp.float32),
        in_specs=[SMEM, VMEM, VMEM, VMEM, FAR, FAR],
        out_specs=VMEM,
        scratch_shapes=[
            pltpu.VMEM((plane // 4, doubled, 4 * bond), jnp.bfloat16),
            pltpu.VMEM((doubled, bits), jnp.bfloat16),
            pltpu.VMEM((rows // 2, doubled), jnp.float32),
            pltpu.VMEM((rows // 2, doubled), jnp.float32),
            pltpu.SemaphoreType.DMA((2,)),
        ],
        compiler_params=pltpu.CompilerParams(vmem_limit_bytes=16 << 20),
        name="amplitudes",
    )(
        core,
        packed_own,
        partners.reshape(plane, cores, bond, doubled),
        owners,
        pltpu.with_memory_space_constraint(received, pltpu.HBM),
        pltpu.with_memory_space_constraint(left_cols, pltpu.HBM),
    )
    across = near // cores
    near_first = [
        (cores - 1 - side) * across + (step + across // 2) % across for side in range(cores) for step in range(across)
    ]
    arrived = lax.all_to_all(
        partial.reshape(near, rows // near, doubled),
        NEAR,
        split_axis=0,
        concat_axis=0,
        tiled=True,
        axis_index_groups=[near_first],
    )
    summed = pl.pallas_call(
        fold_kernel,
        out_shape=jax.ShapeDtypeStruct((plane // columns, columns, doubled), jnp.float32),
        in_specs=[VMEM],
        out_specs=VMEM,
        name="fold",
    )(pltpu.with_memory_space_constraint(arrived, pltpu.VMEM))
    far_first = [
        (row + half) % (2 * half) * columns + (column + columns // 2) % columns
        for row in range(2 * half)
        for column in range(columns)
    ]
    arrived = lax.all_to_all(
        summed.reshape(plane, doubled),
        PLANE,
        split_axis=0,
        concat_axis=0,
        tiled=True,
        axis_index_groups=[far_first],
    )
    return pl.pallas_call(
        finish_kernel,
        out_shape=jax.ShapeDtypeStruct((2, per), jnp.float32),
        in_specs=[SMEM, VMEM],
        out_specs=VMEM,
        name="finish",
    )(place, pltpu.with_memory_space_constraint(arrived, pltpu.VMEM))


def solution(mesh):
    torus = Mesh(
        mesh.devices.reshape(8, 8, 2, mesh.shape["batch"]), ("cuts_0", "cuts_1", "cuts_2", "batch")
    )
    in_specs = (
        P(CUTS_BATCH, None, None),
        P(CUTS_BATCH, None, None),
        P(),
        P(CUTS_BATCH, None, None),
        P(CUTS_BATCH, None),
        P(CUTS_BATCH, None),
        P(),
        P(),
        P(),
    )
    out_specs = P(None, CUTS_BATCH)
    return jax.shard_map(
        on_device, mesh=torus, in_specs=in_specs, out_specs=out_specs, check_vma=False
    )
```

```python
import jax
import jax.numpy as jnp
from jax import lax
from jax.experimental import pallas as pl
from jax.experimental.pallas import tpu as pltpu
from jax.sharding import Mesh
from jax.sharding import PartitionSpec as P

CUTS = ("cuts_0", "cuts_1", "cuts_2")
CUTS_BATCH = ("cuts_0", "cuts_1", "cuts_2", "batch")
PLANE = ("cuts_0", "cuts_1")
NEAR = ("cuts_2", "batch")
TOGETHER = 8
PARTS = 2


def lower_half(shape):
    return lax.broadcasted_iota(jnp.int32, shape, len(shape) - 1) < shape[-1] // 2


def times_i(matrix):
    turned = pltpu.roll(matrix, matrix.shape[-1] // 2, axis=matrix.ndim - 1)
    return jnp.where(lower_half(matrix.shape), -turned, turned)


def advance_kernel(
    core, levels, sending, blocks, selectors, layers, left, right, owners,
    packed_other, packed_own, left_cols, tables,
):
    depth, bond, doubled = layers.shape
    pairs = blocks.shape[0] // 2
    for layer in range(depth):
        plain = layers[layer].astype(jnp.float32)
        turned = times_i(plain)
        tables[layer, :bond, :doubled] = plain.astype(jnp.bfloat16)
        tables[layer, :bond, doubled:] = turned.astype(jnp.bfloat16)
        tables[layer, bond:, :doubled] = turned.astype(jnp.bfloat16)
        tables[layer, bond:, doubled:] = (-plain).astype(jnp.bfloat16)

    plain = right[...].astype(jnp.float32)
    packed_own[pairs // 4, :, :doubled] = jnp.concatenate([plain, times_i(plain)], axis=0).astype(jnp.bfloat16)
    left_rows = jnp.concatenate([left[:, :bond], left[:, bond:]], axis=0)
    width = 512

    def columns(step, carry):
        at = pl.ds(pl.multiple_of(step * width, width), width)
        owner = owners[:, at]
        codes = lax.broadcasted_iota(jnp.int32, (bond, width), 0)
        by_left = jnp.where(codes == owner // bond, 1.0, 0.0).astype(jnp.bfloat16)
        left_cols[:, at] = jnp.dot(left_rows, by_left, preferred_element_type=jnp.float32).astype(jnp.bfloat16)
        return carry

    lax.fori_loop(0, owners.shape[1] // width, columns, 0)

    def group(index, carry, side, packed):
        first = index * TOGETHER
        slot = [sending[0, (first + k) * 2 + side] for k in range(TOGETHER)]
        level = [levels[0, slot[k]] for k in range(TOGETHER)]
        current = [blocks[slot[k]] for k in range(TOGETHER)]
        straight, crossed = [], []
        for k in range(TOGETHER):
            factor = selectors[slot[k]].astype(jnp.float32)
            swapped = pltpu.roll(factor, bond, axis=1)
            mask = lower_half(factor.shape)
            straight.append(jnp.where(mask, factor, swapped))
            crossed.append(jnp.where(mask, swapped, factor))
        for layer in range(depth):
            product = jnp.dot(
                jnp.concatenate(current, axis=0), tables[layer], preferred_element_type=jnp.float32
            )
            for k in range(TOGETHER):
                rows = product[k * bond : (k + 1) * bond]
                updated = (
                    rows[:, :doubled] * straight[k][layer : layer + 1]
                    + rows[:, doubled:] * crossed[k][layer : layer + 1]
                )
                current[k] = lax.select(level[k] > layer, updated.astype(jnp.bfloat16), current[k])
        mask = lower_half((bond, doubled))
        for k in range(0, TOGETHER, 2):
            one = current[k].astype(jnp.float32)
            two = current[k + 1].astype(jnp.float32)
            real = jnp.where(mask, one, pltpu.roll(two, bond, axis=1)).astype(jnp.bfloat16)
            imag = jnp.where(mask, pltpu.roll(one, bond, axis=1), two).astype(jnp.bfloat16)
            quad, part = divmod(k, 4)
            lanes = slice(part * bond, part * bond + doubled)
            packed[index * (TOGETHER // 4) + quad, :bond, lanes] = real
            packed[index * (TOGETHER // 4) + quad, bond:, lanes] = imag
        return carry

    steps = pairs // TOGETHER
    lax.fori_loop(0, steps, lambda i, c: group(i, c, 1 - core[0], packed_other), 0)
    lax.fori_loop(0, steps, lambda i, c: group(i, c, core[0], packed_own), 0)


def split(matrix):
    high = matrix.astype(jnp.bfloat16)
    return high, (matrix - high.astype(jnp.float32)).astype(jnp.bfloat16)


def amplitude_kernel(
    core, own, partners, owners, other_far, left_far, partial,
    other, left_cols, real_rows, imag_rows, arrivals, *, scale,
):
    quads, doubled, depth = other.shape
    bond = doubled // 2
    for far, near, arrival in ((other_far, other, 0), (left_far, left_cols, 1)):
        each = near.shape[0] // PARTS
        for part in range(PARTS):
            at = pl.ds(part * each, each)
            pltpu.make_async_copy(far.at[at], near.at[at], arrivals.at[arrival]).start()
    total = jnp.zeros((doubled, doubled), jnp.float32)
    for worked, side in ((own, core[0]), (other, 1 - core[0])):
        if worked is other:
            pltpu.make_async_copy(other_far, other, arrivals.at[0]).wait()
        for quad in range(quads):
            rows = jnp.concatenate([partners[quad * 4 + k, side] for k in range(4)], axis=0)
            total = total + jnp.dot(worked[quad], rows, preferred_element_type=jnp.float32)
    whole = (total[:bond] + times_i(total[bond:])) * scale
    factors = own[quads, :, :doubled]
    waves = jnp.dot(jnp.concatenate(split(whole), axis=0), factors, preferred_element_type=jnp.float32)
    wave = waves[:bond] + waves[bond:]
    high, low = split(jnp.concatenate([wave, times_i(wave)], axis=0))
    pieces = jnp.concatenate([high.astype(jnp.float32), low.astype(jnp.float32)], axis=0).T.astype(jnp.bfloat16)
    width = 512
    pltpu.make_async_copy(left_far, left_cols, arrivals.at[1]).wait()
    for start in range(0, left_cols.shape[1], width):
        cols = left_cols[:, start : start + width]
        half = jnp.dot(pieces, jnp.concatenate([cols, cols], axis=0), preferred_element_type=jnp.float32)
        codes = lax.broadcasted_iota(jnp.int32, (bond, width), 0)
        chosen = codes == owners[:, start : start + width] % bond
        real = jnp.sum(jnp.where(chosen, half[:bond], 0.0), axis=0, keepdims=True)
        imag = jnp.sum(jnp.where(chosen, half[bond:], 0.0), axis=0, keepdims=True)
        for tile in range(width // 128):
            row = start // 128 + tile
            real_rows[row : row + 1, :] = real[:, tile * 128 : (tile + 1) * 128]
            imag_rows[row : row + 1, :] = imag[:, tile * 128 : (tile + 1) * 128]
    real, imag = real_rows[...], imag_rows[...]
    first = lax.broadcasted_iota(jnp.int32, real.shape, 1) % 16 < 8
    half_rows = real.shape[0]
    partial[:half_rows] = jnp.where(first, real, pltpu.roll(imag, 8, axis=1))
    partial[half_rows:] = jnp.where(first, pltpu.roll(real, 120, axis=1), imag)


def fold_kernel(arrived, summed):
    total = jnp.sum(arrived[...], axis=0)
    summed[...] = jnp.broadcast_to(total[:, None, :], summed.shape)


def finish_kernel(place, arrived, out):
    total = jnp.broadcast_to(jnp.sum(arrived[...], axis=0, keepdims=True), (8, 128))
    total = pltpu.roll(total, (128 - 16 * place[0]) % 128, axis=1)
    out[0:1, :] = total[0:1, 0:8]
    out[1:2, :] = total[0:1, 8:16]


VMEM = pl.BlockSpec(memory_space=pltpu.VMEM)
SMEM = pl.BlockSpec(memory_space=pltpu.SMEM)
FAR = pl.BlockSpec(memory_space=pltpu.HBM)


def on_device(
    blocks, environments, layers, selectors, classes, routing, left_edges, right_edges, owner_map
):
    slots, bond, doubled = blocks.shape
    depth = layers.shape[0]
    bits = owner_map.shape[0]
    near = lax.axis_size(NEAR)
    plane = lax.axis_size(PLANE)
    cores = lax.axis_size("cuts_2")
    partners = lax.all_to_all(
        environments.reshape(plane, cores * bond, doubled), PLANE, split_axis=0, concat_axis=0, tiled=True
    )
    core = lax.axis_index("cuts_2").reshape(1).astype(jnp.int32)
    place = lax.axis_index("cuts_1").reshape(1).astype(jnp.int32)
    per = bits // (near * plane)
    columns = lax.axis_size("cuts_1")
    half = plane // columns // 2
    owners = owner_map.reshape(2, half * columns * near * per)[::-1]
    owners = owners.reshape(plane, 2 * cores, near // cores // 2 * per)[:, ::-1]
    owners = owners.reshape(plane // columns, columns, near, per).transpose(2, 0, 1, 3)
    owners = owners.reshape(2, plane // 2, columns, per).transpose(1, 2, 0, 3).reshape(1, bits)
    core, place, owners = lax.optimization_barrier((core, place, owners))
    packed_other, packed_own, left_cols = pl.pallas_call(
        advance_kernel,
        out_shape=(
            jax.ShapeDtypeStruct((plane // 4, doubled, 4 * bond), jnp.bfloat16),
            jax.ShapeDtypeStruct((plane // 4 + 1, doubled, 4 * bond), jnp.bfloat16),
            jax.ShapeDtypeStruct((doubled, bits), jnp.bfloat16),
        ),
        in_specs=[SMEM] * 3 + [VMEM] * 6,
        out_specs=(VMEM,) * 3,
        scratch_shapes=[pltpu.VMEM((depth, doubled, 2 * doubled), jnp.bfloat16)],
        compiler_params=pltpu.CompilerParams(vmem_limit_bytes=16 << 20),
        name="advance",
    )(core, classes, routing, blocks, selectors, layers, left_edges, right_edges, owners)
    received = lax.ppermute(packed_other, "cuts_2", [(0, 1), (1, 0)])
    rows = bits * 2 // doubled
    scale = float(slots * near * plane) ** -0.5
    partial = pl.pallas_call(
        lambda *refs: amplitude_kernel(*refs, scale=scale),
        out_shape=jax.ShapeDtypeStruct((rows, doubled), jnp.float32),
        in_specs=[SMEM, VMEM, VMEM, VMEM, FAR, FAR],
        out_specs=VMEM,
        scratch_shapes=[
            pltpu.VMEM((plane // 4, doubled, 4 * bond), jnp.bfloat16),
            pltpu.VMEM((doubled, bits), jnp.bfloat16),
            pltpu.VMEM((rows // 2, doubled), jnp.float32),
            pltpu.VMEM((rows // 2, doubled), jnp.float32),
            pltpu.SemaphoreType.DMA((2,)),
        ],
        compiler_params=pltpu.CompilerParams(vmem_limit_bytes=16 << 20),
        name="amplitudes",
    )(
        core,
        packed_own,
        partners.reshape(plane, cores, bond, doubled),
        owners,
        pltpu.with_memory_space_constraint(received, pltpu.HBM),
        pltpu.with_memory_space_constraint(left_cols, pltpu.HBM),
    )
    across = near // cores
    near_first = [
        (cores - 1 - side) * across + (step + across // 2) % across for side in range(cores) for step in range(across)
    ]
    arrived = lax.all_to_all(
        partial.reshape(near, rows // near, doubled),
        NEAR,
        split_axis=0,
        concat_axis=0,
        tiled=True,
        axis_index_groups=[near_first],
    )
    summed = pl.pallas_call(
        fold_kernel,
        out_shape=jax.ShapeDtypeStruct((plane // columns, columns, doubled), jnp.float32),
        in_specs=[VMEM],
        out_specs=VMEM,
        name="fold",
    )(pltpu.with_memory_space_constraint(arrived, pltpu.VMEM))
    far_first = [
        (row + half) % (2 * half) * columns + (column + columns // 2) % columns
        for row in range(2 * half)
        for column in range(columns)
    ]
    arrived = lax.all_to_all(
        summed.reshape(plane, doubled),
        PLANE,
        split_axis=0,
        concat_axis=0,
        tiled=True,
        axis_index_groups=[far_first],
    )
    return pl.pallas_call(
        finish_kernel,
        out_shape=jax.ShapeDtypeStruct((2, per), jnp.float32),
        in_specs=[SMEM, VMEM],
        out_specs=VMEM,
        name="finish",
    )(place, pltpu.with_memory_space_constraint(arrived, pltpu.VMEM))


def solution(mesh):
    torus = Mesh(
        mesh.devices.reshape(8, 8, 2, mesh.shape["batch"]), ("cuts_0", "cuts_1", "cuts_2", "batch")
    )
    in_specs = (
        P(CUTS_BATCH, None, None),
        P(CUTS_BATCH, None, None),
        P(),
        P(CUTS_BATCH, None, None),
        P(CUTS_BATCH, None),
        P(CUTS_BATCH, None),
        P(),
        P(),
        P(),
    )
    out_specs = P(None, CUTS_BATCH)
    return jax.shard_map(
        on_device, mesh=torus, in_specs=in_specs, out_specs=out_specs, check_vma=False
    )
```
